256 devices in a mesh: frac: 16 (over z, y_hi), rock: 16 (over y_lo, x, core).
Axes of the slice: x: 4, y: 4 (y_hi: 2, y_lo: 2; y = y_hi * 2 + y_lo), z: 8, core: 2. Of those that a mesh axis runs over, the one named last changes fastest.
Arguments:
- frac_conc: bfloat16 [512, 1024, 128], P(('frac', 'rock')), may hold values from -6 to 6
- frac_len: int32 [512], P(('frac', 'rock')), may hold values from 256 to 1024, as said below
- frac_flux: bfloat16 [512, 1024, 1024], P(('frac', 'rock')), may hold values from -0.1875 to 0.1875
- frac_inverse: bfloat16 [512, 1024, 1024], P(('frac', 'rock')), may hold values from -0.1875 to 0.1875
- inter_rows: int32 [16, 16, 16, 32], P('frac', 'rock'), may hold values from -1 to 2047, as said below
- wall_rows: int32 [16, 16, 16, 32], P('frac', 'rock'), may hold values from -1 to 2047, as said below
- wall_cells: int32 [16, 16, 16, 32], P('frac', 'rock'), may hold values from -1 to 2047, as said below
- rock_conc: float32 [128, 256, 2048], P(None, 'rock', 'frac'), may hold values from 0.05 to 4
- rock_diff: float32 [256, 2048], P('rock', 'frac'), may hold values from 0.5 to 1
- comp_rate: float32 [128], replicated, may hold values from 0.1 to 0.24
- cross_rate: float32 [128], replicated, may hold values from 0.1 to 0.8
- wall_rate: float32 [128], replicated, may hold values from 0.1 to 0.5
- sorb_cap: float32 [128], replicated, may hold values from 0.2 to 2
- sorb_aff: float32 [128], replicated, may hold values from 0.2 to 2
Outputs:
- frac_final: bfloat16 [512, 1024, 128], P(('frac', 'rock'))
- rock_final: float32 [128, 256, 2048], P(None, 'rock', 'frac')
The draws below stay inside these ranges and needn't reach their ends.
Inputs may be any that keep to these rules, and one draw needn't show every extreme that they name: `frac_len`: one fracture has exactly 1024 live nodes. `inter_rows`: each entry is -1 or a live node row of device (f, r); entry [f, r, p, s] is live exactly when entry [p, r, f, s] is, and the two are one intersection; entries with p = f are -1; some device has 32 live entries towards some peer. `wall_rows`: each entry is -1 or a live node row of device (f, r); entry [f, r, q, s] is live exactly when wall_cells[f, q, r, s] is, and the two are one wall contact. `wall_cells`: each entry is -1 or a cell number of device (f, q)'s tile; for every f some q receives 32 live slots from every r; several slots may name one cell.
All inputs are finite; a program needn't handle non-finite values.
Results may differ from the reference program's by a relative error of at most 0.0064.
Values may be sent and summed in bfloat16 or wider, within the bound.
A program may use at most 64 MiB of HBM per device.

```python
import math
import jax
import jax.numpy as jnp
from jax import lax

COMPONENTS = 128
NODES = 1024
FD = 2
TX = 16
TY = 128
CAP = 32
WCAP = 32
STEPS = 2
FRACS = 512
GX = 256
GY = 2048
N_FRAC = 16
N_ROCK = 16


def fracture_lengths(key):
    drawn = jax.random.randint(jax.random.fold_in(key, 11), (FRACS,), NODES // 4, NODES + 1)
    return drawn.at[0].set(NODES).astype(jnp.int32)


def draw_frac_len(key, part):
    return fracture_lengths(key)


def live_rows(key, salt_value, device_index, array_shape):
    slot_index = jax.random.randint(jax.random.fold_in(key, salt_value), array_shape, 0, FD)
    raw_bits = jax.random.randint(jax.random.fold_in(key, salt_value + 1), array_shape, 0, 1 << 20)
    length = fracture_lengths(key)[device_index * FD + slot_index]
    return (slot_index * NODES + raw_bits % length).astype(jnp.int32)


def draw_inter_rows(key, part):
    array_shape = (N_FRAC, N_ROCK, N_FRAC, CAP)
    counts = jax.random.randint(jax.random.fold_in(key, 21), (N_ROCK, N_FRAC, N_FRAC), 0, CAP + 1)
    counts = jnp.maximum(counts, jnp.transpose(counts, (0, 2, 1)))
    counts = counts.at[:, 0, 1].set(CAP).at[:, 1, 0].set(CAP)
    counts = jnp.where(jnp.eye(N_FRAC, dtype=bool)[None], 0, counts)
    counts = jnp.transpose(counts, (1, 0, 2))
    frac_index = lax.broadcasted_iota(jnp.int32, array_shape, 0)
    rock_index = lax.broadcasted_iota(jnp.int32, array_shape, 1)
    slot_index = lax.broadcasted_iota(jnp.int32, array_shape, 3)
    row_values = live_rows(key, 23, frac_index * N_ROCK + rock_index, array_shape)
    return jnp.where(slot_index < counts[..., None], row_values, -1).astype(jnp.int32)


def wall_counts(key):
    counts = jax.random.randint(jax.random.fold_in(key, 31), (N_FRAC, N_ROCK, N_ROCK), 0, WCAP + 1)
    busiest = jax.random.randint(jax.random.fold_in(key, 32), (N_FRAC,), 0, N_ROCK)
    target = lax.broadcasted_iota(jnp.int32, (N_FRAC, N_ROCK, N_ROCK), 2)
    return jnp.where(target == busiest[:, None, None], WCAP, counts)


def draw_wall_rows(key, part):
    array_shape = (N_FRAC, N_ROCK, N_ROCK, WCAP)
    counts = wall_counts(key)
    frac_index = lax.broadcasted_iota(jnp.int32, array_shape, 0)
    source_index = lax.broadcasted_iota(jnp.int32, array_shape, 1)
    slot_index = lax.broadcasted_iota(jnp.int32, array_shape, 3)
    row_values = live_rows(key, 33, frac_index * N_ROCK + source_index, array_shape)
    return jnp.where(slot_index < counts[..., None], row_values, -1).astype(jnp.int32)


def draw_wall_cells(key, part):
    array_shape = (N_FRAC, N_ROCK, N_ROCK, WCAP)
    counts = jnp.transpose(wall_counts(key), (0, 2, 1))
    slot_index = lax.broadcasted_iota(jnp.int32, array_shape, 3)
    cell_values = jax.random.randint(jax.random.fold_in(key, 35), array_shape, 0, TX * TY)
    return jnp.where(slot_index < counts[..., None], cell_values, -1).astype(jnp.int32)


def steps_of(stream_key, dims, shards, low, high):
    def one(dim, blocks):
        heights = jax.random.uniform(jax.random.fold_in(jax.random.fold_in(stream_key, 6), dim), (blocks,), jnp.float32, low / len(shards), high / len(shards))
        return jnp.repeat(jnp.exp(heights), dims[dim] // blocks).reshape((-1,) + (1,) * (len(dims) - dim - 1))

    gain = one(*shards[0])
    for cut in shards[1:]:
        gain = gain * one(*cut)
    return gain


def scatter_about(rng, extent, scale, reach, cuts=(), kind=jnp.bfloat16):
    entries = scale * jax.random.normal(rng, extent, jnp.float32)
    if cuts:
        entries = entries * steps_of(rng, extent, cuts, -0.22, 0.18)
    return jnp.clip(entries, -reach, reach).astype(kind)


def setup_inputs(seed: int = 0) -> dict:
    arg_keys = jax.random.split(jax.random.key(seed), 15)
    return {
        "frac_conc": scatter_about(arg_keys[0], (FRACS, NODES, COMPONENTS), 1.0, 6.0, ((0, 256),)),
        "frac_len": draw_frac_len(jax.random.fold_in(arg_keys[14], 71), 0),
        "frac_flux": scatter_about(arg_keys[2], (FRACS, NODES, NODES), NODES ** -0.5, 0.1875, ((0, 256),)),
        "frac_inverse": scatter_about(arg_keys[3], (FRACS, NODES, NODES), NODES ** -0.5, 0.1875, ((0, 256),)),
        "inter_rows": draw_inter_rows(jax.random.fold_in(arg_keys[14], 71), 0),
        "wall_rows": draw_wall_rows(jax.random.fold_in(arg_keys[14], 71), 0),
        "wall_cells": draw_wall_cells(jax.random.fold_in(arg_keys[14], 71), 0),
        "rock_conc": jnp.clip(jnp.exp(math.log(4.0) - 4.3820266 * jax.random.uniform(arg_keys[7], (COMPONENTS, GX, GY), jnp.float32) ** steps_of(arg_keys[7], (COMPONENTS, GX, GY), ((1, 16), (2, 16)), -0.2, 0.2)), 0.05, 4.0),
        "rock_diff": jnp.clip(jnp.exp(math.log(1.0) - 0.6931472 * jax.random.uniform(arg_keys[8], (GX, GY), jnp.float32) ** steps_of(arg_keys[8], (GX, GY), ((0, 16), (1, 16)), -0.2, 0.2)), 0.5, 1.0),
        "comp_rate": jnp.clip(jnp.exp(jax.random.uniform(arg_keys[9], (COMPONENTS,), jnp.float32, math.log(0.1), math.log(0.24))), 0.1, 0.24),
        "cross_rate": jnp.clip(jnp.exp(jax.random.uniform(arg_keys[10], (COMPONENTS,), jnp.float32, math.log(0.1), math.log(0.8))), 0.1, 0.8),
        "wall_rate": jnp.clip(jnp.exp(jax.random.uniform(arg_keys[11], (COMPONENTS,), jnp.float32, math.log(0.1), math.log(0.5))), 0.1, 0.5),
        "sorb_cap": jnp.clip(jnp.exp(jax.random.uniform(arg_keys[12], (COMPONENTS,), jnp.float32, math.log(0.2), math.log(2.0))), 0.2, 2.0),
        "sorb_aff": jnp.clip(jnp.exp(jax.random.uniform(arg_keys[13], (COMPONENTS,), jnp.float32, math.log(0.2), math.log(2.0))), 0.2, 2.0),
    }


def neighbour_sum(padded_field, padded_diff, centre_field, centre_diff):
    extent_x = centre_field.shape[1]
    extent_y = centre_field.shape[2]
    running = jnp.zeros_like(centre_field)
    for offset_x, offset_y in ((0, 1), (2, 1), (1, 0), (1, 2)):
        neighbour = padded_field[:, offset_x:offset_x + extent_x, offset_y:offset_y + extent_y]
        neighbour_diff = padded_diff[offset_x:offset_x + extent_x, offset_y:offset_y + extent_y]
        running = running + jnp.sqrt(centre_diff * neighbour_diff) * (neighbour - centre_field)
    return running

def retardation(field, sorb_cap, sorb_aff):
    return 1.0 + sorb_cap[:, None, None] / jnp.square(1.0 + sorb_aff[:, None, None] * jnp.abs(field))

def fracture_step(operands):
    flux_op, inverse_op, conc_one, source_one, mask_one = operands
    carried = jnp.dot(flux_op, conc_one, preferred_element_type=jnp.float32)
    mixed = (conc_one.astype(jnp.float32) + carried + source_one).astype(jnp.bfloat16)
    solved = jnp.dot(inverse_op, mixed, preferred_element_type=jnp.float32)
    return jnp.where(mask_one, solved, 0.0).astype(jnp.bfloat16)

def reference(frac_conc, frac_len, frac_flux, frac_inverse, inter_rows, wall_rows, wall_cells, rock_conc, rock_diff, comp_rate, cross_rate, wall_rate, sorb_cap, sorb_aff):
    slot_rows = FD * NODES
    tile_cells = TX * TY
    node_mask = (jnp.arange(NODES, dtype=jnp.int32)[None, :] < frac_len[:, None])[:, :, None]
    zero_half = jnp.zeros((), jnp.bfloat16)
    concentration = jnp.where(node_mask, frac_conc, zero_half)
    rock_field = rock_conc
    padded_diff = jnp.pad(rock_diff, 1)
    frac_column = jnp.arange(N_FRAC, dtype=jnp.int32)[:, None, None]
    rock_column = jnp.arange(N_ROCK, dtype=jnp.int32)[:, None, None]
    for step_index in range(STEPS):
        by_device = concentration.reshape(N_FRAC, N_ROCK, slot_rows, COMPONENTS)

        def crossing(rock_index):
            pair_rows = inter_rows[:, rock_index]
            pair_live = (pair_rows >= 0)[..., None]
            pair_clip = jnp.maximum(pair_rows, 0)
            own_values = jnp.where(pair_live, by_device[:, rock_index][frac_column, pair_clip], zero_half)
            remote_values = jnp.transpose(own_values, (1, 0, 2, 3))
            cross_flux = jnp.where(pair_live, cross_rate * (remote_values.astype(jnp.float32) - own_values.astype(jnp.float32)), 0.0)
            return jnp.zeros((N_FRAC, slot_rows, COMPONENTS), jnp.float32).at[frac_column, pair_clip].add(cross_flux)
        inflow = jnp.transpose(lax.map(crossing, jnp.arange(N_ROCK, dtype=jnp.int32)), (1, 0, 2, 3))
        rock_tiles = jnp.transpose(rock_field.reshape(COMPONENTS, N_ROCK, TX, N_FRAC, TY), (3, 1, 2, 4, 0)).reshape(N_FRAC, N_ROCK, tile_cells, COMPONENTS)

        def walls(frac_index):
            source_rows = wall_rows[frac_index]
            target_cells = wall_cells[frac_index]
            row_live = (source_rows >= 0)[..., None]
            row_clip = jnp.maximum(source_rows, 0)
            cell_live = (target_cells >= 0)[..., None]
            cell_clip = jnp.maximum(target_cells, 0)
            fracture_side = jnp.where(row_live, by_device[frac_index][rock_column, row_clip], zero_half)
            rock_side = rock_tiles[frac_index][rock_column, cell_clip].astype(jnp.bfloat16)
            wall_flux = jnp.where(cell_live, wall_rate * (jnp.transpose(fracture_side, (1, 0, 2, 3)).astype(jnp.float32) - rock_side.astype(jnp.float32)), 0.0)
            gained = jnp.zeros((N_ROCK, tile_cells, COMPONENTS), jnp.float32).at[rock_column, cell_clip].add(wall_flux)
            lost = jnp.zeros((N_ROCK, slot_rows, COMPONENTS), jnp.float32).at[rock_column, row_clip].add(jnp.transpose(wall_flux, (1, 0, 2, 3)))
            return (gained, lost)
        gained, lost = lax.map(walls, jnp.arange(N_FRAC, dtype=jnp.int32))
        wall_gain = jnp.transpose(gained.reshape(N_FRAC, N_ROCK, TX, TY, COMPONENTS), (4, 1, 2, 0, 3)).reshape(COMPONENTS, N_ROCK * TX, N_FRAC * TY)
        padded_field = jnp.pad(rock_field, ((0, 0), (1, 1), (1, 1)))
        diffusion = comp_rate[:, None, None] * neighbour_sum(padded_field, padded_diff, rock_field, rock_diff)
        rock_field = rock_field + (diffusion + wall_gain) / retardation(rock_field, sorb_cap, sorb_aff)
        source = (inflow - lost).reshape(FRACS, NODES, COMPONENTS)
        concentration = lax.map(fracture_step, (frac_flux, frac_inverse, concentration, source, node_mask))
    return (concentration, rock_field)
```

```python
import functools

import jax
import jax.numpy as jnp
from jax import lax
from jax.experimental import pallas as pl
from jax.experimental.pallas import tpu as pltpu
from jax.sharding import PartitionSpec as P

STEPS = 2
N = 16
CAP = 32
C = 128
NODES = 1024
TX = 16
TY = 128
F32 = jnp.float32
BF16 = jnp.bfloat16
MESH = pl.DeviceIdType.MESH
BLK = 256


def rows(b, size):
    return pl.ds(pl.multiple_of(b * size, size), size)


def one_hot(hit):
    return jnp.where(hit, 1.0, 0.0).astype(BF16)


def decode(v):
    return jnp.where(v < 0, -1, v & (NODES - 1))


def kernel(
    conc_h,
    len_s,
    flux_h,
    inv_h,
    inter_v,
    wall_v,
    cells_v,
    rock_h,
    diff_v,
    comp_v,
    cross_v,
    wrate_v,
    cap_v,
    aff_v,
    conc_o,
    rock_o,
    conc_in,
    flux_v,
    inv_v,
    rock_in,
    conc2,
    mixed2,
    acc,
    table,
    idxb,
    rowb,
    g_op,
    gt_op,
    r_op,
    rt_op,
    f2,
    fr2,
    send_f,
    recv_f,
    send_r,
    recv_w,
    r_ref,
    rock2,
    s_bc,
    t_bc,
    w_ref,
    gain,
    dh,
    ye,
    yh,
    yeb,
    yhb,
    xeb,
    xhb,
    load_sem,
    x_send,
    x_recv,
    w_send,
    w_recv,
    v_send,
    v_recv,
    h_send,
    h_recv,
):
    me_f = lax.axis_index("frac")
    me_r = lax.axis_index("rock")

    loads = [
        pltpu.make_async_copy(src, dst, load_sem.at[i])
        for i, (src, dst) in enumerate(
            ((conc_h, conc_in), (rock_h, rock_in), (flux_h, flux_v), (inv_h, inv_v))
        )
    ]
    for load in loads:
        load.start()

    barrier = pltpu.get_barrier_semaphore()

    def greet(k, carry):
        pl.semaphore_signal(
            barrier, inc=1, device_id=(lax.rem(me_f + k, N), me_r), device_id_type=MESH
        )
        pl.semaphore_signal(
            barrier, inc=1, device_id=(me_f, lax.rem(me_r + k, N)), device_id_type=MESH
        )
        return carry

    lax.fori_loop(1, N, greet, 0)

    def x_copy(step, peer, slot):
        return pltpu.make_async_remote_copy(
            src_ref=send_f.at[step, peer],
            dst_ref=recv_f.at[step, slot],
            send_sem=x_send.at[step, peer],
            recv_sem=x_recv.at[step, slot],
            device_id=(peer, me_r),
            device_id_type=MESH,
        )

    def w_copy(step, peer, slot):
        return pltpu.make_async_remote_copy(
            src_ref=send_f.at[step, N + peer],
            dst_ref=recv_w.at[step, slot],
            send_sem=w_send.at[step, peer],
            recv_sem=w_recv.at[step, slot],
            device_id=(me_f, peer),
            device_id_type=MESH,
        )

    def v_copy(step, peer, slot):
        return pltpu.make_async_remote_copy(
            src_ref=send_r.at[step, peer],
            dst_ref=recv_f.at[step, N + slot],
            send_sem=v_send.at[step, peer],
            recv_sem=v_recv.at[step, slot],
            device_id=(me_f, peer),
            device_id_type=MESH,
        )

    def each_peer(me, act):
        def turn(k, carry):
            act(lax.rem(me + k, N))
            return carry

        lax.fori_loop(1, N, turn, 0)

    before_f = lax.rem(me_f + N - 1, N)
    after_f = lax.rem(me_f + 1, N)
    before_r = lax.rem(me_r + N - 1, N)
    after_r = lax.rem(me_r + 1, N)
    sides = (
        ((me_f, after_r), 0),
        ((me_f, before_r), 1),
        ((after_f, me_r), 2),
        ((before_f, me_r), 3),
    )

    def diff_copies():
        return [
            pltpu.make_async_remote_copy(
                src_ref=diff_v,
                dst_ref=dh.at[side],
                send_sem=h_send.at[0, side],
                recv_sem=h_recv.at[0, side],
                device_id=device,
                device_id_type=MESH,
            )
            for device, side in sides
        ]

    def halo_copies(step):
        out = []
        for device, side in sides:
            src, dst = (xeb, xhb) if side < 2 else (yeb, yhb)
            out.append(
                pltpu.make_async_remote_copy(
                    src_ref=src.at[step, side % 2],
                    dst_ref=dst.at[step, side % 2],
                    send_sem=h_send.at[1 + step, side],
                    recv_sem=h_recv.at[1 + step, side],
                    device_id=device,
                    device_id_type=MESH,
                )
            )
        return out

    table[...] = jnp.zeros_like(table)
    table[0:N, 0:CAP] = inter_v[...].astype(F32)
    table[N : 2 * N, 0:CAP] = wall_v[...].astype(F32)
    table[2 * N : 3 * N, 0:CAP] = cells_v[...].astype(F32)
    turned = jnp.transpose(table[...])
    for k in range(3 * N):
        idxb[k * CAP : (k + 1) * CAP, :] = jnp.broadcast_to(
            turned[0:CAP, k : k + 1], (CAP, C)
        ).astype(jnp.int32)

    lane = lax.broadcasted_iota(jnp.int32, (128, 128), 1)
    sub = lax.broadcasted_iota(jnp.int32, (128, 128), 0)

    def build_gather(op, first, count):
        def turn(b, carry):
            node = decode(idxb[rows(b + first, 128), :])
            for h in range(NODES // 128):
                op[rows(b, 128), h * 128 : (h + 1) * 128] = one_hot(node == lane + h * 128)
            return carry

        lax.fori_loop(0, count, turn, 0)

    def build_scatter(op, first, count):
        def turn(b, carry):
            for j in range(count):
                node = jnp.broadcast_to(
                    rowb[(first + j) * 8 : (first + j) * 8 + 1, :], (128, 128)
                )
                op[rows(b, 128), j * 128 : (j + 1) * 128] = one_hot(node == sub + b * 128)
            return carry

        lax.fori_loop(0, NODES // 128, turn, 0)

    build_gather(g_op, 0, 8)

    loads[0].wait()

    def mask_turn(b, carry):
        node = lax.broadcasted_iota(jnp.int32, (BLK, C), 0) + b * BLK
        for a in range(2):
            value = conc_in[a, rows(b, BLK), :].astype(F32)
            conc2[rows(b, BLK), a * C : (a + 1) * C] = jnp.where(
                node < len_s[a], value, 0.0
            ).astype(BF16)
        return carry

    lax.fori_loop(0, NODES // BLK, mask_turn, 0)

    def gather(op, source, first, dest, step, count):
        def turn(b, carry):
            found = jnp.dot(op[rows(b, BLK), :], source[...], preferred_element_type=F32)
            high = idxb[pl.ds(pl.multiple_of(first + b * BLK, 128), BLK), :] >= NODES
            own = jnp.where(high, found[:, C:], found[:, :C]).astype(BF16)
            dest[step, pl.ds(b * (BLK // CAP), BLK // CAP)] = own.reshape(BLK // CAP, CAP, C)
            return carry

        lax.fori_loop(0, count, turn, 0)

    def send_fractures(step):
        each_peer(me_f, lambda peer: x_copy(step, peer, me_f).start())
        each_peer(me_r, lambda peer: w_copy(step, peer, me_r).start())
        recv_f[step, me_f] = send_f[step, me_f]
        recv_w[step, me_r] = send_f[step, N + me_r]

    def send_rock(step):
        each_peer(me_r, lambda peer: v_copy(step, peer, me_r).start())
        for copy in halo_copies(step):
            copy.start()
        recv_f[step, N + me_r] = send_r[step, me_r]

    gather(g_op, conc2, 0, send_f, 0, 4)
    pl.semaphore_wait(barrier, 2 * (N - 1))
    for copy in diff_copies():
        copy.start()
    send_fractures(0)

    s_here = jnp.sqrt(diff_v[...])
    table[0:TX, :] = s_here
    turned = jnp.transpose(table[...])
    for x in range(TX):
        s_bc[x] = jnp.broadcast_to(turned[:, x : x + 1], (TY, C))

    def put_state(step, x, state):
        scaled = s_bc[x] * state
        r_ref[x] = state
        w_ref[step, x + 1, 8 : 8 + TY, :] = scaled
        ye[0, pl.ds(x, 1), :] = scaled[TY - 1 :, :]
        ye[1, pl.ds(x, 1), :] = scaled[:1, :]
        half = x // 8
        low = x % 8
        return half, low, state.astype(BF16)

    def edges(step):
        yeb[step] = ye[...].astype(BF16)
        xeb[step, 0] = w_ref[step, TX, 8 : 8 + TY, :].astype(BF16)
        xeb[step, 1] = w_ref[step, 1, 8 : 8 + TY, :].astype(BF16)

    loads[1].wait()
    for x in range(TX):
        half, low, small = put_state(0, x, jnp.transpose(rock_in[:, x, :]))
        rock2[low * TY : (low + 1) * TY, half * C : (half + 1) * C] = small
    edges(0)
    build_gather(r_op, 8, 4)
    gather(r_op, rock2, 2 * N * CAP, send_r, 0, 2)
    send_rock(0)

    for j in range(12):
        row = jnp.zeros((8, 128), F32)
        kind, first = divmod(4 * j, N)
        source = (inter_v, wall_v, cells_v)[kind]
        pieces = [source[first + i : first + i + 1, :] for i in range(4)]
        rowb[j * 8 : j * 8 + 1, :] = decode(jnp.concatenate(pieces, axis=1))
    build_scatter(gt_op, 0, 8)
    build_scatter(rt_op, 8, 4)

    def product():
        for a in range(2):

            def turn(b, carry):
                acc[a, rows(b, BLK), :] = conc2[rows(b, BLK), a * C : (a + 1) * C].astype(
                    F32
                ) + jnp.dot(
                    flux_v[a, rows(b, BLK), :],
                    conc2[:, a * C : (a + 1) * C],
                    preferred_element_type=F32,
                )
                return carry

            lax.fori_loop(0, NODES // BLK, turn, 0)

    loads[2].wait()
    product()

    for copy in diff_copies():
        copy.wait_recv()
    xrow = lax.broadcasted_iota(jnp.int32, (TX, TY), 0)
    ycol = lax.broadcasted_iota(jnp.int32, (TX, TY), 1)
    side_s = jnp.sqrt(dh[...])
    first_r, last_r = me_r == 0, me_r == N - 1
    first_f, last_f = me_f == 0, me_f == N - 1
    down_x = jnp.where(first_r, 0.0, side_s[0, TX - 1 :, :])
    up_x = jnp.where(last_r, 0.0, side_s[1, :1, :])
    down_y = jnp.where(first_f, 0.0, pltpu.roll(side_s[2], 1, 1))
    up_y = jnp.where(last_f, 0.0, pltpu.roll(side_s[3], TY - 1, 1))
    total = jnp.where(xrow == 0, down_x, pltpu.roll(s_here, 1, 0))
    total = total + jnp.where(xrow == TX - 1, up_x, pltpu.roll(s_here, TX - 1, 0))
    total = total + jnp.where(ycol == 0, down_y, pltpu.roll(s_here, 1, 1))
    total = total + jnp.where(ycol == TY - 1, up_y, pltpu.roll(s_here, TY - 1, 1))
    table[0:TX, :] = s_here * total
    turned = jnp.transpose(table[...])
    for x in range(TX):
        t_bc[x] = jnp.broadcast_to(turned[:, x : x + 1], (TY, C))

    cross_rate = cross_v[...]
    wall_rate = wrate_v[...]

    def flux_of(recv, send, dest, step, first, count):
        def turn(p, carry):
            rate = jnp.where(p < N, cross_rate, wall_rate) if first == 0 else wall_rate
            value = rate * (recv[step, p].astype(F32) - send[step, p].astype(F32))
            high = idxb[rows(first + p, CAP), :] >= NODES
            dest[rows(p, CAP), :C] = jnp.where(high, 0.0, value).astype(BF16)
            dest[rows(p, CAP), C:] = jnp.where(high, value, 0.0).astype(BF16)
            return carry

        lax.fori_loop(0, count, turn, 0)

    def solve(step):
        each_peer(me_f, lambda peer: x_copy(step, peer, peer).wait_recv())
        each_peer(me_r, lambda peer: v_copy(step, peer, peer).wait_recv())
        flux_of(recv_f, send_f, f2, step, 0, 2 * N)

        def mix(b, carry):
            inflow = jnp.dot(gt_op[rows(b, BLK), :], f2[...], preferred_element_type=F32)
            for a in range(2):
                mixed2[rows(b, BLK), a * C : (a + 1) * C] = (
                    acc[a, rows(b, BLK), :] + inflow[:, a * C : (a + 1) * C]
                ).astype(BF16)
            return carry

        lax.fori_loop(0, NODES // BLK, mix, 0)
        if step == 0:
            loads[3].wait()
        for a in range(2):

            def turn(b, carry):
                solved = jnp.dot(
                    inv_v[a, rows(b, BLK), :],
                    mixed2[:, a * C : (a + 1) * C],
                    preferred_element_type=F32,
                )
                node = lax.broadcasted_iota(jnp.int32, (BLK, C), 0) + b * BLK
                solved = jnp.where(node < len_s[a], solved, 0.0).astype(BF16)
                if step == STEPS - 1:
                    conc_o[a, rows(b, BLK), :] = solved
                else:
                    conc2[rows(b, BLK), a * C : (a + 1) * C] = solved
                return carry

            lax.fori_loop(0, NODES // BLK, turn, 0)

    comp_rate = comp_v[...]
    cap = cap_v[...]
    aff = aff_v[...]

    def diffuse(step):
        each_peer(me_r, lambda peer: w_copy(step, peer, peer).wait_recv())
        flux_of(recv_w, send_r, fr2, step, 2 * N, N)

        def spread(b, carry):
            gain[rows(b, BLK), :] = jnp.dot(
                rt_op[rows(b, BLK), :], fr2[...], preferred_element_type=F32
            )
            return carry

        lax.fori_loop(0, NODES // BLK, spread, 0)
        for copy in halo_copies(step):
            copy.wait_recv()
        w_ref[step, 0, 8 : 8 + TY, :] = jnp.where(first_r, 0.0, xhb[step, 0].astype(F32))
        w_ref[step, TX + 1, 8 : 8 + TY, :] = jnp.where(last_r, 0.0, xhb[step, 1].astype(F32))
        yh[0] = jnp.where(first_f, 0.0, yhb[step, 0].astype(F32))
        yh[1] = jnp.where(last_f, 0.0, yhb[step, 1].astype(F32))
        for x in range(TX):
            w_ref[step, x + 1, 7:8, :] = yh[0, x : x + 1, :]
            w_ref[step, x + 1, 8 + TY : 9 + TY, :] = yh[1, x : x + 1, :]
        for x in range(TX):
            half, low = divmod(x, 8)
            old = r_ref[x]
            around = (w_ref[step, x, 8 : 8 + TY, :] + w_ref[step, x + 2, 8 : 8 + TY, :]) + (
                w_ref[step, x + 1, 7 : 7 + TY, :] + w_ref[step, x + 1, 9 : 9 + TY, :]
            )
            diffusion = comp_rate * (s_bc[x] * around - t_bc[x] * old)
            added = diffusion + gain[low * TY : (low + 1) * TY, half * C : (half + 1) * C]
            root = 1.0 + aff * jnp.abs(old)
            square = root * root
            new = old + added * square / (square + cap)
            if step == STEPS - 1:
                rock_o[:, x, :] = jnp.transpose(new)
            else:
                _, _, small = put_state(step + 1, x, new)
                rock2[low * TY : (low + 1) * TY, half * C : (half + 1) * C] = small

    solve(0)
    gather(g_op, conc2, 0, send_f, 1, 4)
    send_fractures(1)
    diffuse(0)
    edges(1)
    gather(r_op, rock2, 2 * N * CAP, send_r, 1, 2)
    send_rock(1)
    product()
    diffuse(1)
    solve(1)

    for copy in diff_copies():
        copy.wait_send()
    for step in range(STEPS):
        each_peer(me_f, lambda peer: x_copy(step, peer, me_f).wait_send())
        each_peer(me_r, lambda peer: w_copy(step, peer, me_r).wait_send())
        each_peer(me_r, lambda peer: v_copy(step, peer, me_r).wait_send())
        for copy in halo_copies(step):
            copy.wait_send()


def local(
    frac_conc,
    frac_len,
    frac_flux,
    frac_inverse,
    inter_rows,
    wall_rows,
    wall_cells,
    rock_conc,
    rock_diff,
    comp_rate,
    cross_rate,
    wall_rate,
    sorb_cap,
    sorb_aff,
):
    any_spec = pl.BlockSpec(memory_space=pl.ANY)
    vmem = pl.BlockSpec(memory_space=pltpu.VMEM)
    smem = pl.BlockSpec(memory_space=pltpu.SMEM)
    dma = pltpu.SemaphoreType.DMA
    V = pltpu.VMEM
    return pl.pallas_call(
        kernel,
        out_shape=(
            jax.ShapeDtypeStruct(frac_conc.shape, BF16),
            jax.ShapeDtypeStruct(rock_conc.shape, F32),
        ),
        in_specs=[any_spec, smem, any_spec, any_spec, vmem, vmem, vmem, any_spec] + [vmem] * 6,
        out_specs=(vmem, vmem),
        scratch_shapes=[
            V((2, NODES, C), BF16),
            V((2, NODES, NODES), BF16),
            V((2, NODES, NODES), BF16),
            V((C, TX, TY), F32),
            V((NODES, 2 * C), BF16),
            V((NODES, 2 * C), BF16),
            V((2, NODES, C), F32),
            V((128, 128), F32),
            V((3 * N * CAP, C), jnp.int32),
            V((12 * 8, 128), jnp.int32),
            V((2 * N * CAP, NODES), BF16),
            V((NODES, 2 * N * CAP), BF16),
            V((N * CAP, NODES), BF16),
            V((NODES, N * CAP), BF16),
            V((2 * N * CAP, 2 * C), BF16),
            V((N * CAP, 2 * C), BF16),
            V((STEPS, 2 * N, CAP, C), BF16),
            V((STEPS, 2 * N, CAP, C), BF16),
            V((STEPS, N, CAP, C), BF16),
            V((STEPS, N, CAP, C), BF16),
            V((TX, TY, C), F32),
            V((NODES, 2 * C), BF16),
            V((TX, TY, C), F32),
            V((TX, TY, C), F32),
            V((STEPS, TX + 2, TY + 16, C), F32),
            V((NODES, 2 * C), F32),
            V((4, TX, TY), F32),
            V((2, TX, C), F32),
            V((2, TX, C), F32),
            V((STEPS, 2, TX, C), BF16),
            V((STEPS, 2, TX, C), BF16),
            V((STEPS, 2, TY, C), BF16),
            V((STEPS, 2, TY, C), BF16),
            dma((4,)),
            dma((STEPS, N)),
            dma((STEPS, N)),
            dma((STEPS, N)),
            dma((STEPS, N)),
            dma((STEPS, N)),
            dma((STEPS, N)),
            dma((STEPS + 1, 4)),
            dma((STEPS + 1, 4)),
        ],
        compiler_params=pltpu.CompilerParams(
            collective_id=0, has_side_effects=True, vmem_limit_bytes=56 << 20
        ),
        name="tracer_steps",
    )(
        frac_conc,
        frac_len,
        frac_flux,
        frac_inverse,
        inter_rows[0, 0],
        wall_rows[0, 0],
        wall_cells[0, 0],
        rock_conc,
        rock_diff,
        comp_rate.reshape(1, C),
        cross_rate.reshape(1, C),
        wall_rate.reshape(1, C),
        sorb_cap.reshape(1, C),
        sorb_aff.reshape(1, C),
    )


def solution(mesh):
    return jax.shard_map(
        local,
        mesh=mesh,
        in_specs=(
            P(("frac", "rock"), None, None),
            P(("frac", "rock")),
            P(("frac", "rock"), None, None),
            P(("frac", "rock"), None, None),
            P("frac", "rock", None, None),
            P("frac", "rock", None, None),
            P("frac", "rock", None, None),
            P(None, "rock", "frac"),
            P("rock", "frac"),
            P(),
            P(),
            P(),
            P(),
            P(),
        ),
        out_specs=(P(("frac", "rock"), None, None), P(None, "rock", "frac")),
        check_vma=False,
    )
```

```python
import functools

import jax
import jax.numpy as jnp
from jax import lax
from jax.experimental import pallas as pl
from jax.experimental.pallas import tpu as pltpu
from jax.sharding import PartitionSpec as P

STEPS = 2
N = 16
CAP = 32
C = 128
NODES = 1024
TX = 16
TY = 128
F32 = jnp.float32
BF16 = jnp.bfloat16
MESH = pl.DeviceIdType.MESH
BLK = 256


def rows(b, size):
    return pl.ds(pl.multiple_of(b * size, size), size)


def one_hot(hit):
    return jnp.where(hit, 1.0, 0.0).astype(BF16)


def decode(v):
    return jnp.where(v < 0, -1, v & (NODES - 1))


def solved_half(inv_v, mixed2, len_s, a):
    solved = jnp.dot(inv_v[a], mixed2[:, a * C : (a + 1) * C], preferred_element_type=F32)
    node = lax.broadcasted_iota(jnp.int32, solved.shape, 0)
    return jnp.where(node < len_s[a], solved, 0.0).astype(BF16)


def kernel(
    conc_h,
    len_h,
    flux_h,
    inv_h,
    inter_h,
    wall_h,
    cells_h,
    rock_h,
    diff_h,
    comp_h,
    cross_h,
    wrate_h,
    cap_h,
    aff_h,
    inv_v,
    mixed2,
    rock_o,
    len_s,
    inter_v,
    wall_v,
    cells_v,
    diff_v,
    comp_v,
    cross_v,
    wrate_v,
    cap_v,
    aff_v,
    conc_in,
    flux_v,
    rock_in,
    conc2,
    acc,
    table,
    idxb,
    rowb,
    g_op,
    gt_op,
    r_op,
    rt_op,
    f2,
    fr2,
    send_f,
    recv_f,
    send_r,
    recv_w,
    r_ref,
    rock2,
    s_bc,
    t_bc,
    w_ref,
    gain,
    dh,
    ye,
    yh,
    edge_out,
    edge_in,
    load_sem,
    x_send,
    x_recv,
    w_send,
    w_recv,
    v_send,
    v_recv,
    h_send,
    h_recv,
    d_send,
    d_recv,
):
    me_f = lax.axis_index("frac")
    me_r = lax.axis_index("rock")

    loads = [
        pltpu.make_async_copy(src, dst, load_sem.at[i])
        for i, (src, dst) in enumerate(
            (
                (conc_h, conc_in),
                (rock_h, rock_in),
                (flux_h, flux_v),
                (inv_h, inv_v),
                (inter_h, inter_v),
                (wall_h, wall_v),
                (cells_h, cells_v),
                (diff_h, diff_v),
                (comp_h, comp_v),
                (cross_h, cross_v),
                (wrate_h, wrate_v),
                (cap_h, cap_v),
                (aff_h, aff_v),
                (len_h, len_s),
            )
        )
    ]
    for i in (4, 5, 0, 13):
        loads[i].start()

    barrier = pltpu.get_barrier_semaphore()

    def greet(k, carry):
        pl.semaphore_signal(
            barrier, inc=1, device_id=(lax.rem(me_f + k, N), me_r), device_id_type=MESH
        )
        pl.semaphore_signal(
            barrier, inc=1, device_id=(me_f, lax.rem(me_r + k, N)), device_id_type=MESH
        )
        return carry

    lax.fori_loop(1, N, greet, 0)
    for i in (6, 7, 1, 2, 3, 8, 9, 10, 11, 12):
        loads[i].start()

    def x_copy(step, peer, slot):
        return pltpu.make_async_remote_copy(
            src_ref=send_f.at[step, peer],
            dst_ref=recv_f.at[step, slot],
            send_sem=x_send.at[step],
            recv_sem=x_recv.at[step],
            device_id=(peer, me_r),
            device_id_type=MESH,
        )

    def w_copy(step, peer, slot):
        return pltpu.make_async_remote_copy(
            src_ref=send_f.at[step, N + peer],
            dst_ref=recv_w.at[step, slot],
            send_sem=w_send.at[step],
            recv_sem=w_recv.at[step],
            device_id=(me_f, peer),
            device_id_type=MESH,
        )

    def v_copy(step, peer, slot):
        return pltpu.make_async_remote_copy(
            src_ref=send_r.at[step, peer],
            dst_ref=recv_f.at[step, N + slot],
            send_sem=v_send.at[step],
            recv_sem=v_recv.at[step],
            device_id=(me_f, peer),
            device_id_type=MESH,
        )

    def each_peer(me, act):
        def turn(k, carry):
            act(lax.rem(me + k, N))
            return carry

        lax.fori_loop(1, N, turn, 0)

    before_f = lax.rem(me_f + N - 1, N)
    after_f = lax.rem(me_f + 1, N)
    before_r = lax.rem(me_r + N - 1, N)
    after_r = lax.rem(me_r + 1, N)
    sides = (
        ((me_f, after_r), 0),
        ((me_f, before_r), 1),
        ((after_f, me_r), 2),
        ((before_f, me_r), 3),
    )

    def diff_copies():
        return [
            pltpu.make_async_remote_copy(
                src_ref=diff_v,
                dst_ref=dh.at[side],
                send_sem=d_send,
                recv_sem=d_recv,
                device_id=device,
                device_id_type=MESH,
            )
            for device, side in sides
        ]

    def halo_copies(step):
        out = []
        for device, side in sides:
            part = (step, side % 2, pl.ds(0, TY) if side < 2 else pl.ds(TY, TX))
            out.append(
                pltpu.make_async_remote_copy(
                    src_ref=edge_out.at[part],
                    dst_ref=edge_in.at[part],
                    send_sem=h_send.at[step],
                    recv_sem=h_recv.at[step],
                    device_id=device,
                    device_id_type=MESH,
                )
            )
        return out

    def drain(ref, sem):
        pltpu.make_async_copy(ref, ref, sem).wait()

    def peers_of(ref, step):
        return ref.at[step, pl.ds(0, N - 1)]

    table[...] = jnp.zeros_like(table)
    loads[4].wait()
    loads[5].wait()
    table[0:N, 0:CAP] = inter_v[...].astype(F32)
    table[N : 2 * N, 0:CAP] = wall_v[...].astype(F32)

    def spread_slots(first, last):
        turned = jnp.transpose(table[...])
        for k in range(first, last):
            idxb[k * CAP : (k + 1) * CAP, :] = jnp.broadcast_to(
                turned[0:CAP, k : k + 1], (CAP, C)
            ).astype(jnp.int32)

    spread_slots(0, 2 * N)

    lane = lax.broadcasted_iota(jnp.int32, (128, 128), 1)
    sub = lax.broadcasted_iota(jnp.int32, (128, 128), 0)

    def build_gather(op, first, count):
        def turn(b, carry):
            node = decode(idxb[rows(b + first, 128), :])
            for h in range(NODES // 128):
                op[rows(b, 128), h * 128 : (h + 1) * 128] = one_hot(node == lane + h * 128)
            return carry

        lax.fori_loop(0, count, turn, 0)

    def build_scatter(op, first, count):
        def turn(b, carry):
            for j in range(count):
                node = jnp.broadcast_to(
                    rowb[(first + j) * 8 : (first + j) * 8 + 1, :], (128, 128)
                )
                op[rows(b, 128), j * 128 : (j + 1) * 128] = one_hot(node == sub + b * 128)
            return carry

        lax.fori_loop(0, NODES // 128, turn, 0)

    build_gather(g_op, 0, 8)

    loads[0].wait()
    loads[13].wait()

    def mask_turn(b, carry):
        node = lax.broadcasted_iota(jnp.int32, (BLK, C), 0) + b * BLK
        for a in range(2):
            value = conc_in[a, rows(b, BLK), :].astype(F32)
            conc2[rows(b, BLK), a * C : (a + 1) * C] = jnp.where(
                node < len_s[a], value, 0.0
            ).astype(BF16)
        return carry

    lax.fori_loop(0, NODES // BLK, mask_turn, 0)

    def gather(op, source, first, dest, step):
        count = op.shape[0]
        found = jnp.dot(op[...], source[...], preferred_element_type=F32)
        high = idxb[first : first + count, :] >= NODES
        own = jnp.where(high, found[:, C:], found[:, :C]).astype(BF16)
        dest[step] = own.reshape(count // CAP, CAP, C)

    def send_fractures(step):
        each_peer(me_f, lambda peer: x_copy(step, peer, me_f).start())
        each_peer(me_r, lambda peer: w_copy(step, peer, me_r).start())
        recv_f[step, me_f] = send_f[step, me_f]
        recv_w[step, me_r] = send_f[step, N + me_r]

    def send_rock(step):
        each_peer(me_r, lambda peer: v_copy(step, peer, me_r).start())
        for copy in halo_copies(step):
            copy.start()
        recv_f[step, N + me_r] = send_r[step, me_r]

    gather(g_op, conc2, 0, send_f, 0)
    loads[7].wait()
    pl.semaphore_wait(barrier, 2 * (N - 1))
    send_fractures(0)
    for copy in diff_copies():
        copy.start()

    loads[6].wait()
    table[2 * N : 3 * N, 0:CAP] = cells_v[...].astype(F32)
    spread_slots(2 * N, 3 * N)

    s_here = jnp.sqrt(diff_v[...])
    table[0:TX, :] = s_here
    turned = jnp.transpose(table[...])
    for x in range(TX):
        s_bc[x] = jnp.broadcast_to(turned[:, x : x + 1], (TY, C))

    def put_state(step, x, state):
        scaled = s_bc[x] * state
        r_ref[x] = state
        w_ref[step, x + 1, 8 : 8 + TY, :] = scaled
        ye[0, pl.ds(x, 1), :] = scaled[TY - 1 :, :]
        ye[1, pl.ds(x, 1), :] = scaled[:1, :]
        half = x // 8
        low = x % 8
        return half, low, state.astype(BF16)

    def edges(step):
        edge_out[step, :, TY:, :] = ye[...].astype(BF16)
        edge_out[step, 0, :TY, :] = w_ref[step, TX, 8 : 8 + TY, :].astype(BF16)
        edge_out[step, 1, :TY, :] = w_ref[step, 1, 8 : 8 + TY, :].astype(BF16)

    loads[1].wait()
    for x in range(TX):
        half, low, small = put_state(0, x, jnp.transpose(rock_in[:, x, :]))
        rock2[low * TY : (low + 1) * TY, half * C : (half + 1) * C] = small
    edges(0)
    build_gather(r_op, 8, 4)
    gather(r_op, rock2, 2 * N * CAP, send_r, 0)
    send_rock(0)

    for j in range(12):
        row = jnp.zeros((8, 128), F32)
        kind, first = divmod(4 * j, N)
        source = (inter_v, wall_v, cells_v)[kind]
        pieces = [source[first + i : first + i + 1, :] for i in range(4)]
        rowb[j * 8 : j * 8 + 1, :] = decode(jnp.concatenate(pieces, axis=1))
    build_scatter(gt_op, 0, 8)
    build_scatter(rt_op, 8, 4)

    def product():
        for a in range(2):
            conc = conc2[:, a * C : (a + 1) * C]
            acc[a] = conc.astype(F32) + jnp.dot(flux_v[a], conc, preferred_element_type=F32)

    loads[2].wait()
    product()

    drain(dh, d_recv)
    xrow = lax.broadcasted_iota(jnp.int32, (TX, TY), 0)
    ycol = lax.broadcasted_iota(jnp.int32, (TX, TY), 1)
    side_s = jnp.sqrt(dh[...])
    first_r, last_r = me_r == 0, me_r == N - 1
    first_f, last_f = me_f == 0, me_f == N - 1
    down_x = jnp.where(first_r, 0.0, side_s[0, TX - 1 :, :])
    up_x = jnp.where(last_r, 0.0, side_s[1, :1, :])
    down_y = jnp.where(first_f, 0.0, pltpu.roll(side_s[2], 1, 1))
    up_y = jnp.where(last_f, 0.0, pltpu.roll(side_s[3], TY - 1, 1))
    total = jnp.where(xrow == 0, down_x, pltpu.roll(s_here, 1, 0))
    total = total + jnp.where(xrow == TX - 1, up_x, pltpu.roll(s_here, TX - 1, 0))
    total = total + jnp.where(ycol == 0, down_y, pltpu.roll(s_here, 1, 1))
    total = total + jnp.where(ycol == TY - 1, up_y, pltpu.roll(s_here, TY - 1, 1))
    table[0:TX, :] = s_here * total
    turned = jnp.transpose(table[...])
    for x in range(TX):
        t_bc[x] = jnp.broadcast_to(turned[:, x : x + 1], (TY, C))

    for i in (8, 9, 10, 11, 12):
        loads[i].wait()
    cross_rate = cross_v[...]
    wall_rate = wrate_v[...]

    def flux_of(recv, send, dest, step, first, count):
        def turn(p, carry):
            rate = jnp.where(p < N, cross_rate, wall_rate) if first == 0 else wall_rate
            value = rate * (recv[step, p].astype(F32) - send[step, p].astype(F32))
            high = idxb[rows(first + p, CAP), :] >= NODES
            dest[rows(p, CAP), :C] = jnp.where(high, 0.0, value).astype(BF16)
            dest[rows(p, CAP), C:] = jnp.where(high, value, 0.0).astype(BF16)
            return carry

        lax.fori_loop(0, count, turn, 0)

    def solve(step):
        drain(peers_of(recv_f, step), x_recv.at[step])
        drain(peers_of(recv_f, step), v_recv.at[step])
        flux_of(recv_f, send_f, f2, step, 0, 2 * N)

        inflow = jnp.dot(gt_op[...], f2[...], preferred_element_type=F32)
        for a in range(2):
            mixed2[:, a * C : (a + 1) * C] = (
                acc[a] + inflow[:, a * C : (a + 1) * C]
            ).astype(BF16)

    def advance():
        loads[3].wait()
        for a in range(2):
            conc2[:, a * C : (a + 1) * C] = solved_half(inv_v, mixed2, len_s, a)

    comp_rate = comp_v[...]
    cap = cap_v[...]
    aff = aff_v[...]

    def diffuse(step):
        drain(peers_of(recv_w, step), w_recv.at[step])
        flux_of(recv_w, send_r, fr2, step, 2 * N, N)
        gain[...] = jnp.dot(rt_op[...], fr2[...], preferred_element_type=F32)
        drain(edge_in.at[step], h_recv.at[step])
        w_ref[step, 0, 8 : 8 + TY, :] = jnp.where(first_r, 0.0, edge_in[step, 0, :TY, :].astype(F32))
        w_ref[step, TX + 1, 8 : 8 + TY, :] = jnp.where(last_r, 0.0, edge_in[step, 1, :TY, :].astype(F32))
        yh[0] = jnp.where(first_f, 0.0, edge_in[step, 0, TY:, :].astype(F32))
        yh[1] = jnp.where(last_f, 0.0, edge_in[step, 1, TY:, :].astype(F32))
        for x in range(TX):
            w_ref[step, x + 1, 7:8, :] = yh[0, x : x + 1, :]
            w_ref[step, x + 1, 8 + TY : 9 + TY, :] = yh[1, x : x + 1, :]
        for x in range(TX):
            half, low = divmod(x, 8)
            old = r_ref[x]
            around = (w_ref[step, x, 8 : 8 + TY, :] + w_ref[step, x + 2, 8 : 8 + TY, :]) + (
                w_ref[step, x + 1, 7 : 7 + TY, :] + w_ref[step, x + 1, 9 : 9 + TY, :]
            )
            diffusion = comp_rate * (s_bc[x] * around - t_bc[x] * old)
            added = diffusion + gain[low * TY : (low + 1) * TY, half * C : (half + 1) * C]
            root = 1.0 + aff * jnp.abs(old)
            square = root * root
            new = old + added * square / (square + cap)
            if step == STEPS - 1:
                rock_o[:, x, :] = jnp.transpose(new)
            else:
                _, _, small = put_state(step + 1, x, new)
                rock2[low * TY : (low + 1) * TY, half * C : (half + 1) * C] = small

    solve(0)
    advance()
    gather(g_op, conc2, 0, send_f, 1)
    send_fractures(1)
    diffuse(0)
    edges(1)
    gather(r_op, rock2, 2 * N * CAP, send_r, 1)
    send_rock(1)
    product()
    diffuse(1)
    solve(1)

    drain(dh, d_send)
    for step in range(STEPS):
        drain(peers_of(send_f, step), x_send.at[step])
        drain(peers_of(send_f, step), w_send.at[step])
        drain(peers_of(send_r, step), v_send.at[step])
        drain(edge_out.at[step], h_send.at[step])


def finish(len_h, inv_v, mixed2, rock_v, conc_h, rock_h, len_s, conc_v, sem):
    rock_copy = pltpu.make_async_copy(rock_v, rock_h, sem.at[2])
    rock_copy.start()
    len_copy = pltpu.make_async_copy(len_h, len_s, sem.at[3])
    len_copy.start()
    len_copy.wait()
    copies = []
    for a in range(2):
        conc_v[a] = solved_half(inv_v, mixed2, len_s, a)
        copies.append(pltpu.make_async_copy(conc_v.at[a], conc_h.at[a], sem.at[a]))
        copies[-1].start()
    for copy in copies:
        copy.wait()
    rock_copy.wait()


def local(
    frac_conc,
    frac_len,
    frac_flux,
    frac_inverse,
    inter_rows,
    wall_rows,
    wall_cells,
    rock_conc,
    rock_diff,
    comp_rate,
    cross_rate,
    wall_rate,
    sorb_cap,
    sorb_aff,
):
    any_spec = pl.BlockSpec(memory_space=pl.ANY)
    vmem = pl.BlockSpec(memory_space=pltpu.VMEM)
    dma = pltpu.SemaphoreType.DMA
    V = pltpu.VMEM
    def stay(x):
        return pltpu.with_memory_space_constraint(x, pltpu.HBM)

    inverse, mixed, rock = pl.pallas_call(
        kernel,
        out_shape=(
            V(frac_inverse.shape, BF16),
            V((NODES, 2 * C), BF16),
            V(rock_conc.shape, F32),
        ),
        in_specs=[any_spec] * 14,
        out_specs=(vmem, vmem, vmem),
        scratch_shapes=[
            pltpu.SMEM((2,), jnp.int32),
            V((N, CAP), jnp.int32),
            V((N, CAP), jnp.int32),
            V((N, CAP), jnp.int32),
            V((TX, TY), F32),
            V((1, C), F32),
            V((1, C), F32),
            V((1, C), F32),
            V((1, C), F32),
            V((1, C), F32),
            V((2, NODES, C), BF16),
            V((2, NODES, NODES), BF16),
            V((C, TX, TY), F32),
            V((NODES, 2 * C), BF16),
            V((2, NODES, C), F32),
            V((128, 128), F32),
            V((3 * N * CAP, C), jnp.int32),
            V((12 * 8, 128), jnp.int32),
            V((2 * N * CAP, NODES), BF16),
            V((NODES, 2 * N * CAP), BF16),
            V((N * CAP, NODES), BF16),
            V((NODES, N * CAP), BF16),
            V((2 * N * CAP, 2 * C), BF16),
            V((N * CAP, 2 * C), BF16),
            V((STEPS, 2 * N, CAP, C), BF16),
            V((STEPS, 2 * N, CAP, C), BF16),
            V((STEPS, N, CAP, C), BF16),
            V((STEPS, N, CAP, C), BF16),
            V((TX, TY, C), F32),
            V((NODES, 2 * C), BF16),
            V((TX, TY, C), F32),
            V((TX, TY, C), F32),
            V((STEPS, TX + 2, TY + 16, C), F32),
            V((NODES, 2 * C), F32),
            V((4, TX, TY), F32),
            V((2, TX, C), F32),
            V((2, TX, C), F32),
            V((STEPS, 2, TY + TX, C), BF16),
            V((STEPS, 2, TY + TX, C), BF16),
            dma((14,)),
            dma((STEPS,)),
            dma((STEPS,)),
            dma((STEPS,)),
            dma((STEPS,)),
            dma((STEPS,)),
            dma((STEPS,)),
            dma((STEPS,)),
            dma((STEPS,)),
            dma(()),
            dma(()),
        ],
        compiler_params=pltpu.CompilerParams(
            collective_id=0, has_side_effects=True, vmem_limit_bytes=36 << 20
        ),
        name="tracer_steps",
    )(
        stay(frac_conc),
        stay(frac_len),
        stay(frac_flux),
        stay(frac_inverse),
        stay(inter_rows[0, 0]),
        stay(wall_rows[0, 0]),
        stay(wall_cells[0, 0]),
        stay(rock_conc),
        stay(rock_diff),
        stay(comp_rate.reshape(1, C)),
        stay(cross_rate.reshape(1, C)),
        stay(wall_rate.reshape(1, C)),
        stay(sorb_cap.reshape(1, C)),
        stay(sorb_aff.reshape(1, C)),
    )
    return pl.pallas_call(
        finish,
        out_shape=(
            jax.ShapeDtypeStruct(frac_conc.shape, BF16),
            jax.ShapeDtypeStruct(rock_conc.shape, F32),
        ),
        in_specs=[any_spec, vmem, vmem, vmem],
        out_specs=(any_spec, any_spec),
        scratch_shapes=[pltpu.SMEM((2,), jnp.int32), V(frac_conc.shape, BF16), dma((4,))],
        compiler_params=pltpu.CompilerParams(vmem_limit_bytes=8 << 20),
        name="finish",
    )(stay(frac_len), inverse, mixed, rock)


def solution(mesh):
    return jax.shard_map(
        local,
        mesh=mesh,
        in_specs=(
            P(("frac", "rock"), None, None),
            P(("frac", "rock")),
            P(("frac", "rock"), None, None),
            P(("frac", "rock"), None, None),
            P("frac", "rock", None, None),
            P("frac", "rock", None, None),
            P("frac", "rock", None, None),
            P(None, "rock", "frac"),
            P("rock", "frac"),
            P(),
            P(),
            P(),
            P(),
            P(),
        ),
        out_specs=(P(("frac", "rock"), None, None), P(None, "rock", "frac")),
        check_vma=False,
    )
```

```python
import functools

import jax
import jax.numpy as jnp
from jax import lax
from jax.experimental import pallas as pl
from jax.experimental.pallas import tpu as pltpu
from jax.sharding import PartitionSpec as P

STEPS = 2
N = 16
CAP = 32
C = 128
NODES = 1024
TX = 16
TY = 128
F32 = jnp.float32
BF16 = jnp.bfloat16
MESH = pl.DeviceIdType.MESH
BLK = 256


def rows(b, size):
    return pl.ds(pl.multiple_of(b * size, size), size)


def one_hot(hit):
    return jnp.where(hit, 1.0, 0.0).astype(BF16)


def decode(v):
    return jnp.where(v < 0, -1, v & (NODES - 1))


FAR_FIRST = sorted(range(1, N), key=lambda k: abs(k - N // 2))


def solved_rows(inv_v, mixed2, lens, a, first, count):
    solved = jnp.dot(
        inv_v[a, first : first + count, :],
        mixed2[:, a * C : (a + 1) * C],
        preferred_element_type=F32,
    )
    node = lax.broadcasted_iota(jnp.int32, (count, C), 0) + first
    return jnp.where(node < lens[a : a + 1, :], solved, 0.0).astype(BF16)


def kernel(
    conc_h,
    len_h,
    flux_h,
    inv_h,
    inter_h,
    wall_h,
    cells_h,
    rock_h,
    diff_h,
    comp_h,
    cross_h,
    wrate_h,
    cap_h,
    aff_h,
    inv_v,
    mixed2,
    rock_o,
    lens,
    len_s,
    inter_v,
    wall_v,
    cells_v,
    diff_v,
    comp_v,
    cross_v,
    wrate_v,
    cap_v,
    aff_v,
    conc_in,
    flux_v,
    rock_in,
    conc2,
    acc,
    table,
    idxb,
    rowb,
    g_op,
    gt_op,
    r_op,
    rt_op,
    f2,
    fr2,
    send_f,
    recv_f,
    send_r,
    recv_w,
    r_ref,
    rock2,
    s_bc,
    t_bc,
    w_ref,
    fac,
    dh,
    ye,
    yh,
    edge_out,
    edge_in,
    load_sem,
    x_send,
    x_recv,
    w_send,
    w_recv,
    v_send,
    v_recv,
    h_send,
    h_recv,
    d_send,
    d_recv,
):
    me_f = lax.axis_index("frac")
    me_r = lax.axis_index("rock")

    loads = [
        pltpu.make_async_copy(src, dst, load_sem.at[i])
        for i, (src, dst) in enumerate(
            (
                (conc_h, conc_in),
                (rock_h, rock_in),
                (flux_h, flux_v),
                (inv_h, inv_v),
                (inter_h, inter_v),
                (wall_h, wall_v),
                (cells_h, cells_v),
                (diff_h, diff_v),
                (comp_h, comp_v),
                (cross_h, cross_v),
                (wrate_h, wrate_v),
                (cap_h, cap_v),
                (aff_h, aff_v),
                (len_h, len_s),
            )
        )
    ]
    barrier = pltpu.get_barrier_semaphore()

    loads[4].start()
    loads[5].start()
    for k in FAR_FIRST:
        pl.semaphore_signal(
            barrier, inc=1, device_id=(lax.rem(me_f + k, N), me_r), device_id_type=MESH
        )
    for k in FAR_FIRST:
        pl.semaphore_signal(
            barrier, inc=1, device_id=(me_f, lax.rem(me_r + k, N)), device_id_type=MESH
        )
    for i in (0, 13, 7, 1, 6, 2, 3, 8, 9, 10, 11, 12):
        loads[i].start()

    def x_copy(step, peer, slot):
        return pltpu.make_async_remote_copy(
            src_ref=send_f.at[step, peer],
            dst_ref=recv_f.at[step, slot],
            send_sem=x_send.at[step],
            recv_sem=x_recv.at[step],
            device_id=(peer, me_r),
            device_id_type=MESH,
        )

    def w_copy(step, peer, slot):
        return pltpu.make_async_remote_copy(
            src_ref=send_f.at[step, N + peer],
            dst_ref=recv_w.at[step, slot],
            send_sem=w_send.at[step],
            recv_sem=w_recv.at[step],
            device_id=(me_f, peer),
            device_id_type=MESH,
        )

    def v_copy(step, peer, slot):
        return pltpu.make_async_remote_copy(
            src_ref=send_r.at[step, peer],
            dst_ref=recv_f.at[step, N + slot],
            send_sem=v_send.at[step],
            recv_sem=v_recv.at[step],
            device_id=(me_f, peer),
            device_id_type=MESH,
        )

    def each_peer(me, act):
        for k in FAR_FIRST:
            act(lax.rem(me + k, N))

    before_f = lax.rem(me_f + N - 1, N)
    after_f = lax.rem(me_f + 1, N)
    before_r = lax.rem(me_r + N - 1, N)
    after_r = lax.rem(me_r + 1, N)
    sides = (
        ((me_f, after_r), 0),
        ((me_f, before_r), 1),
        ((after_f, me_r), 2),
        ((before_f, me_r), 3),
    )

    def diff_copies():
        return [
            pltpu.make_async_remote_copy(
                src_ref=diff_v,
                dst_ref=dh.at[side],
                send_sem=d_send,
                recv_sem=d_recv,
                device_id=device,
                device_id_type=MESH,
            )
            for device, side in sides
        ]

    def halo_copies(step):
        out = []
        for device, side in sides:
            part = (step, side % 2, pl.ds(0, TY) if side < 2 else pl.ds(TY, TX))
            out.append(
                pltpu.make_async_remote_copy(
                    src_ref=edge_out.at[part],
                    dst_ref=edge_in.at[part],
                    send_sem=h_send.at[step],
                    recv_sem=h_recv.at[step],
                    device_id=device,
                    device_id_type=MESH,
                )
            )
        return out

    def drain(ref, sem):
        pltpu.make_async_copy(ref, ref, sem).wait()

    def peers_of(ref, step):
        return ref.at[step, pl.ds(0, N - 1)]

    table[...] = jnp.zeros_like(table)
    loads[4].wait()
    loads[5].wait()
    table[0:N, 0:CAP] = inter_v[...].astype(F32)
    table[N : 2 * N, 0:CAP] = wall_v[...].astype(F32)

    def spread_slots(first, last):
        turned = jnp.transpose(table[...])
        for k in range(first, last):
            idxb[k * CAP : (k + 1) * CAP, :] = jnp.broadcast_to(
                turned[0:CAP, k : k + 1], (CAP, C)
            ).astype(jnp.int32)

    spread_slots(0, 2 * N)

    lane = lax.broadcasted_iota(jnp.int32, (128, 128), 1)
    sub = lax.broadcasted_iota(jnp.int32, (128, 128), 0)

    def build_gather(op, first, count):
        def turn(b, carry):
            node = decode(idxb[rows(b + first, 128), :])
            for h in range(NODES // 128):
                op[rows(b, 128), h * 128 : (h + 1) * 128] = one_hot(node == lane + h * 128)
            return carry

        lax.fori_loop(0, count, turn, 0)

    def build_scatter(op, first, count):
        def turn(b, carry):
            for j in range(count):
                node = jnp.broadcast_to(
                    rowb[(first + j) * 8 : (first + j) * 8 + 1, :], (128, 128)
                )
                op[rows(b, 128), j * 128 : (j + 1) * 128] = one_hot(node == sub + b * 128)
            return carry

        lax.fori_loop(0, NODES // 128, turn, 0)

    build_gather(g_op, 0, 8)

    loads[0].wait()
    loads[13].wait()
    for a in range(2):
        lens[a : a + 1, :] = jnp.full((1, C), len_s[a], jnp.int32)

    def mask_turn(b, carry):
        node = lax.broadcasted_iota(jnp.int32, (BLK, C), 0) + b * BLK
        for a in range(2):
            value = conc_in[a, rows(b, BLK), :].astype(F32)
            conc2[rows(b, BLK), a * C : (a + 1) * C] = jnp.where(
                node < len_s[a], value, 0.0
            ).astype(BF16)
        return carry

    lax.fori_loop(0, NODES // BLK, mask_turn, 0)

    def gather(op, source, first, dest, step, part):
        for begin in range(part * N * CAP, (part + 1) * N * CAP, BLK):
            found = jnp.dot(op[begin : begin + BLK, :], source[...], preferred_element_type=F32)
            high = idxb[first + begin : first + begin + BLK, :] >= NODES
            own = jnp.where(high, found[:, C:], found[:, :C]).astype(BF16)
            dest[step, begin // CAP : (begin + BLK) // CAP] = own.reshape(BLK // CAP, CAP, C)

    def send_crossing(step):
        each_peer(me_f, lambda peer: x_copy(step, peer, me_f).start())
        recv_f[step, me_f] = send_f[step, me_f]

    def send_walls(step):
        each_peer(me_r, lambda peer: w_copy(step, peer, me_r).start())
        recv_w[step, me_r] = send_f[step, N + me_r]

    def send_rock(step):
        each_peer(me_r, lambda peer: v_copy(step, peer, me_r).start())
        recv_f[step, N + me_r] = send_r[step, me_r]

    gather(g_op, conc2, 0, send_f, 0, 0)
    gather(g_op, conc2, 0, send_f, 0, 1)
    loads[7].wait()

    s_here = jnp.sqrt(diff_v[...])
    table[0:TX, :] = s_here
    turned = jnp.transpose(table[...])
    for x in range(TX):
        s_bc[x] = jnp.broadcast_to(turned[:, x : x + 1], (TY, C))

    def put_state(step, x, state):
        scaled = s_bc[x] * state
        r_ref[x] = state
        w_ref[step, x + 1, 8 : 8 + TY, :] = scaled
        ye[0, pl.ds(x, 1), :] = scaled[TY - 1 :, :]
        ye[1, pl.ds(x, 1), :] = scaled[:1, :]
        half, low = divmod(x, 8)
        rock2[low * TY : (low + 1) * TY, half * C : (half + 1) * C] = state.astype(BF16)

    def edges(step):
        edge_out[step, :, TY:, :] = ye[...].astype(BF16)
        edge_out[step, 0, :TY, :] = w_ref[step, TX, 8 : 8 + TY, :].astype(BF16)
        edge_out[step, 1, :TY, :] = w_ref[step, 1, 8 : 8 + TY, :].astype(BF16)

    loads[1].wait()
    for x in range(TX):
        put_state(0, x, jnp.transpose(rock_in[:, x, :]))
    edges(0)

    pl.semaphore_wait(barrier, 2 * (N - 1))
    for copy in diff_copies() + halo_copies(0):
        copy.start()
    send_crossing(0)
    send_walls(0)
    loads[6].wait()
    table[2 * N : 3 * N, 0:CAP] = cells_v[...].astype(F32)
    spread_slots(2 * N, 3 * N)
    build_gather(r_op, 8, 4)
    gather(r_op, rock2, 2 * N * CAP, send_r, 0, 0)
    send_rock(0)

    for j in range(12):
        row = jnp.zeros((8, 128), F32)
        kind, first = divmod(4 * j, N)
        source = (inter_v, wall_v, cells_v)[kind]
        pieces = [source[first + i : first + i + 1, :] for i in range(4)]
        rowb[j * 8 : j * 8 + 1, :] = decode(jnp.concatenate(pieces, axis=1))
    build_scatter(rt_op, 8, 4)
    build_scatter(gt_op, 0, 8)

    def product():
        for a in range(2):
            conc = conc2[:, a * C : (a + 1) * C]
            for first in range(0, NODES, BLK):
                part = slice(first, first + BLK)
                acc[a, part, :] = conc[part, :].astype(F32) + jnp.dot(
                    flux_v[a, part, :], conc, preferred_element_type=F32
                )

    loads[2].wait()
    product()

    drain(dh, d_recv)
    xrow = lax.broadcasted_iota(jnp.int32, (TX, TY), 0)
    ycol = lax.broadcasted_iota(jnp.int32, (TX, TY), 1)
    side_s = jnp.sqrt(dh[...])
    first_r, last_r = me_r == 0, me_r == N - 1
    first_f, last_f = me_f == 0, me_f == N - 1
    down_x = jnp.where(first_r, 0.0, side_s[0, TX - 1 :, :])
    up_x = jnp.where(last_r, 0.0, side_s[1, :1, :])
    down_y = jnp.where(first_f, 0.0, pltpu.roll(side_s[2], 1, 1))
    up_y = jnp.where(last_f, 0.0, pltpu.roll(side_s[3], TY - 1, 1))
    total = jnp.where(xrow == 0, down_x, pltpu.roll(s_here, 1, 0))
    total = total + jnp.where(xrow == TX - 1, up_x, pltpu.roll(s_here, TX - 1, 0))
    total = total + jnp.where(ycol == 0, down_y, pltpu.roll(s_here, 1, 1))
    total = total + jnp.where(ycol == TY - 1, up_y, pltpu.roll(s_here, TY - 1, 1))
    table[0:TX, :] = s_here * total
    turned = jnp.transpose(table[...])
    for x in range(TX):
        t_bc[x] = jnp.broadcast_to(turned[:, x : x + 1], (TY, C))

    for i in (8, 9, 10, 11, 12):
        loads[i].wait()
    cross_rate = cross_v[...]
    wall_rate = wrate_v[...]

    def flux_of(rate, recv, send, dest, step, first, begin):
        def turn(p, carry):
            value = rate * (recv[step, p].astype(F32) - send[step, p].astype(F32))
            high = idxb[rows(first + p, CAP), :] >= NODES
            dest[rows(p, CAP), :C] = jnp.where(high, 0.0, value).astype(BF16)
            dest[rows(p, CAP), C:] = jnp.where(high, value, 0.0).astype(BF16)
            return carry

        lax.fori_loop(begin, begin + N, turn, 0)

    def inflow(begin):
        for first in range(0, NODES, BLK):
            part = slice(first, first + BLK)
            slots = slice(begin * CAP, (begin + N) * CAP)
            came = jnp.dot(gt_op[part, slots], f2[slots, :], preferred_element_type=F32)
            for a in range(2):
                total = acc[a, part, :] + came[:, a * C : (a + 1) * C]
                if begin:
                    acc[a, part, :] = total
                else:
                    mixed2[part, a * C : (a + 1) * C] = total.astype(BF16)

    def solve_walls(step):
        drain(peers_of(recv_f, step), v_recv.at[step])
        flux_of(wall_rate, recv_f, send_f, f2, step, 0, N)
        inflow(N)

    def solve_crossing(step):
        drain(peers_of(recv_f, step), x_recv.at[step])
        flux_of(cross_rate, recv_f, send_f, f2, step, 0, 0)
        inflow(0)

    def advance():
        loads[3].wait()
        for a in range(2):
            for first in range(0, NODES, BLK):
                conc2[first : first + BLK, a * C : (a + 1) * C] = solved_rows(
                    inv_v, mixed2, lens, a, first, BLK
                )

    comp_rate = comp_v[...]
    cap = cap_v[...]
    aff = aff_v[...]

    def stencil(step):
        drain(edge_in.at[step], h_recv.at[step])
        w_ref[step, 0, 8 : 8 + TY, :] = jnp.where(first_r, 0.0, edge_in[step, 0, :TY, :].astype(F32))
        w_ref[step, TX + 1, 8 : 8 + TY, :] = jnp.where(last_r, 0.0, edge_in[step, 1, :TY, :].astype(F32))
        yh[0] = jnp.where(first_f, 0.0, edge_in[step, 0, TY:, :].astype(F32))
        yh[1] = jnp.where(last_f, 0.0, edge_in[step, 1, TY:, :].astype(F32))
        for x in range(TX):
            w_ref[step, x + 1, 7:8, :] = yh[0, x : x + 1, :]
            w_ref[step, x + 1, 8 + TY : 9 + TY, :] = yh[1, x : x + 1, :]
        for x in range(TX):
            old = r_ref[x]
            around = (w_ref[step, x, 8 : 8 + TY, :] + w_ref[step, x + 2, 8 : 8 + TY, :]) + (
                w_ref[step, x + 1, 7 : 7 + TY, :] + w_ref[step, x + 1, 9 : 9 + TY, :]
            )
            diffusion = comp_rate * (s_bc[x] * around - t_bc[x] * old)
            root = 1.0 + aff * jnp.abs(old)
            square = root * root
            share = square / (square + cap)
            r_ref[x] = old + diffusion * share
            fac[x] = share

    def absorb(step):
        drain(peers_of(recv_w, step), w_recv.at[step])
        flux_of(wall_rate, recv_w, send_r, fr2, step, 2 * N, 0)
        for low in range(0, 8, 2):
            gain = jnp.dot(
                rt_op[low * TY : (low + 2) * TY, :], fr2[...], preferred_element_type=F32
            )
            for half in range(2):
                for i in range(2):
                    x = half * 8 + low + i
                    new = r_ref[x] + fac[x] * gain[
                        i * TY : (i + 1) * TY, half * C : (half + 1) * C
                    ]
                    if step == STEPS - 1:
                        rock_o[:, x, :] = jnp.transpose(new)
                    else:
                        put_state(step + 1, x, new)

    stencil(0)
    absorb(0)
    edges(1)
    for copy in halo_copies(1):
        copy.start()
    gather(r_op, rock2, 2 * N * CAP, send_r, 1, 0)
    send_rock(1)
    solve_walls(0)
    solve_crossing(0)
    advance()
    gather(g_op, conc2, 0, send_f, 1, 0)
    send_crossing(1)
    gather(g_op, conc2, 0, send_f, 1, 1)
    send_walls(1)
    product()
    stencil(1)
    solve_walls(1)
    absorb(1)
    solve_crossing(1)

    drain(dh, d_send)
    for step in range(STEPS):
        drain(peers_of(send_f, step), x_send.at[step])
        drain(peers_of(send_f, step), w_send.at[step])
        drain(peers_of(send_r, step), v_send.at[step])
        drain(edge_out.at[step], h_send.at[step])


def finish(inv_v, mixed2, rock_v, lens, conc_h, rock_h, conc_v, sem):
    rock_copy = pltpu.make_async_copy(rock_v, rock_h, sem.at[0])
    rock_copy.start()
    copies = [rock_copy]
    for a in range(2):
        for first in range(0, NODES, BLK):
            part = (a, pl.ds(first, BLK))
            conc_v[a, first : first + BLK, :] = solved_rows(inv_v, mixed2, lens, a, first, BLK)
            copies.append(
                pltpu.make_async_copy(conc_v.at[part], conc_h.at[part], sem.at[len(copies)])
            )
            copies[-1].start()
    for copy in copies:
        copy.wait()


def local(
    frac_conc,
    frac_len,
    frac_flux,
    frac_inverse,
    inter_rows,
    wall_rows,
    wall_cells,
    rock_conc,
    rock_diff,
    comp_rate,
    cross_rate,
    wall_rate,
    sorb_cap,
    sorb_aff,
):
    any_spec = pl.BlockSpec(memory_space=pl.ANY)
    vmem = pl.BlockSpec(memory_space=pltpu.VMEM)
    dma = pltpu.SemaphoreType.DMA
    V = pltpu.VMEM
    def stay(x):
        return pltpu.with_memory_space_constraint(x, pltpu.HBM)

    inverse, mixed, rock, lens = pl.pallas_call(
        kernel,
        out_shape=(
            V(frac_inverse.shape, BF16),
            V((NODES, 2 * C), BF16),
            V(rock_conc.shape, F32),
            V((8, C), jnp.int32),
        ),
        in_specs=[any_spec] * 14,
        out_specs=(vmem, vmem, vmem, vmem),
        scratch_shapes=[
            pltpu.SMEM((2,), jnp.int32),
            V((N, CAP), jnp.int32),
            V((N, CAP), jnp.int32),
            V((N, CAP), jnp.int32),
            V((TX, TY), F32),
            V((1, C), F32),
            V((1, C), F32),
            V((1, C), F32),
            V((1, C), F32),
            V((1, C), F32),
            V((2, NODES, C), BF16),
            V((2, NODES, NODES), BF16),
            V((C, TX, TY), F32),
            V((NODES, 2 * C), BF16),
            V((2, NODES, C), F32),
            V((128, 128), F32),
            V((3 * N * CAP, C), jnp.int32),
            V((12 * 8, 128), jnp.int32),
            V((2 * N * CAP, NODES), BF16),
            V((NODES, 2 * N * CAP), BF16),
            V((N * CAP, NODES), BF16),
            V((NODES, N * CAP), BF16),
            V((2 * N * CAP, 2 * C), BF16),
            V((N * CAP, 2 * C), BF16),
            V((STEPS, 2 * N, CAP, C), BF16),
            V((STEPS, 2 * N, CAP, C), BF16),
            V((STEPS, N, CAP, C), BF16),
            V((STEPS, N, CAP, C), BF16),
            V((TX, TY, C), F32),
            V((NODES, 2 * C), BF16),
            V((TX, TY, C), F32),
            V((TX, TY, C), F32),
            V((STEPS, TX + 2, TY + 16, C), F32),
            V((TX, TY, C), F32),
            V((4, TX, TY), F32),
            V((2, TX, C), F32),
            V((2, TX, C), F32),
            V((STEPS, 2, TY + TX, C), BF16),
            V((STEPS, 2, TY + TX, C), BF16),
            dma((14,)),
            dma((STEPS,)),
            dma((STEPS,)),
            dma((STEPS,)),
            dma((STEPS,)),
            dma((STEPS,)),
            dma((STEPS,)),
            dma((STEPS,)),
            dma((STEPS,)),
            dma(()),
            dma(()),
        ],
        compiler_params=pltpu.CompilerParams(
            collective_id=0, has_side_effects=True, vmem_limit_bytes=36 << 20
        ),
        name="tracer_steps",
    )(
        stay(frac_conc),
        stay(frac_len),
        stay(frac_flux),
        stay(frac_inverse),
        stay(inter_rows[0, 0]),
        stay(wall_rows[0, 0]),
        stay(wall_cells[0, 0]),
        stay(rock_conc),
        stay(rock_diff),
        stay(comp_rate.reshape(1, C)),
        stay(cross_rate.reshape(1, C)),
        stay(wall_rate.reshape(1, C)),
        stay(sorb_cap.reshape(1, C)),
        stay(sorb_aff.reshape(1, C)),
    )
    return pl.pallas_call(
        finish,
        out_shape=(
            jax.ShapeDtypeStruct(frac_conc.shape, BF16),
            jax.ShapeDtypeStruct(rock_conc.shape, F32),
        ),
        in_specs=[vmem, vmem, vmem, vmem],
        out_specs=(any_spec, any_spec),
        scratch_shapes=[V(frac_conc.shape, BF16), dma((1 + 2 * NODES // BLK,))],
        compiler_params=pltpu.CompilerParams(vmem_limit_bytes=8 << 20),
        name="finish",
    )(inverse, mixed, rock, lens)


def solution(mesh):
    return jax.shard_map(
        local,
        mesh=mesh,
        in_specs=(
            P(("frac", "rock"), None, None),
            P(("frac", "rock")),
            P(("frac", "rock"), None, None),
            P(("frac", "rock"), None, None),
            P("frac", "rock", None, None),
            P("frac", "rock", None, None),
            P("frac", "rock", None, None),
            P(None, "rock", "frac"),
            P("rock", "frac"),
            P(),
            P(),
            P(),
            P(),
            P(),
        ),
        out_specs=(P(("frac", "rock"), None, None), P(None, "rock", "frac")),
        check_vma=False,
    )
```

```python
import functools

import jax
import jax.numpy as jnp
from jax import lax
from jax.experimental import pallas as pl
from jax.experimental.pallas import tpu as pltpu
from jax.sharding import PartitionSpec as P

STEPS = 2
N = 16
CAP = 32
C = 128
NODES = 1024
TX = 16
TY = 128
F32 = jnp.float32
BF16 = jnp.bfloat16
MESH = pl.DeviceIdType.MESH
BLK = 256


def rows(b, size):
    return pl.ds(pl.multiple_of(b * size, size), size)


def one_hot(hit):
    return jnp.where(hit, 1.0, 0.0).astype(BF16)


def decode(v):
    return jnp.where(v < 0, -1, v & (NODES - 1))


FAR_FIRST = sorted(range(1, N), key=lambda k: abs(k - N // 2))


def solved_rows(inv_v, mixed2, lens, a, first, count):
    solved = jnp.dot(
        inv_v[a, first : first + count, :],
        mixed2[:, a * C : (a + 1) * C],
        preferred_element_type=F32,
    )
    node = lax.broadcasted_iota(jnp.int32, (count, C), 0) + first
    return jnp.where(node < lens[a : a + 1, :], solved, 0.0).astype(BF16)


def absorbed(rt_op, fr2, r_ref, fac, low):
    gain = jnp.dot(rt_op[low * TY : (low + 2) * TY, :], fr2[...], preferred_element_type=F32)
    for half in range(2):
        for i in range(2):
            x = half * 8 + low + i
            brought = gain[i * TY : (i + 1) * TY, half * C : (half + 1) * C]
            yield x, r_ref[x] + fac[x] * brought


def kernel(
    conc_h,
    len_h,
    flux_h,
    inv_h,
    inter_h,
    wall_h,
    cells_h,
    rock_h,
    diff_h,
    comp_h,
    cross_h,
    wrate_h,
    cap_h,
    aff_h,
    inv_v,
    mixed2,
    lens,
    r_ref,
    fac,
    fr2,
    rt_op,
    len_s,
    inter_v,
    wall_v,
    cells_v,
    diff_v,
    comp_v,
    cross_v,
    wrate_v,
    cap_v,
    aff_v,
    conc_in,
    flux_v,
    rock_in,
    conc2,
    acc,
    table,
    idxb,
    rowb,
    g_op,
    gt_op,
    r_op,
    f2,
    send_f,
    recv_f,
    send_r,
    recv_w,
    rock2,
    s_bc,
    t_bc,
    w_ref,
    dh,
    ye,
    yh,
    edge_out,
    edge_in,
    load_sem,
    x_send,
    x_recv,
    w_send,
    w_recv,
    v_send,
    v_recv,
    h_send,
    h_recv,
    d_send,
    d_recv,
):
    me_f = lax.axis_index("frac")
    me_r = lax.axis_index("rock")

    loads = [
        pltpu.make_async_copy(src, dst, load_sem.at[i])
        for i, (src, dst) in enumerate(
            (
                (conc_h, conc_in),
                (rock_h, rock_in),
                (flux_h, flux_v),
                (inv_h, inv_v),
                (inter_h, inter_v),
                (wall_h, wall_v),
                (cells_h, cells_v),
                (diff_h, diff_v),
                (comp_h, comp_v),
                (cross_h, cross_v),
                (wrate_h, wrate_v),
                (cap_h, cap_v),
                (aff_h, aff_v),
                (len_h, len_s),
            )
        )
    ]
    barrier = pltpu.get_barrier_semaphore()

    loads[4].start()
    loads[5].start()
    for k in FAR_FIRST:
        pl.semaphore_signal(
            barrier, inc=1, device_id=(lax.rem(me_f + k, N), me_r), device_id_type=MESH
        )
    for k in FAR_FIRST:
        pl.semaphore_signal(
            barrier, inc=1, device_id=(me_f, lax.rem(me_r + k, N)), device_id_type=MESH
        )
    for i in (0, 13, 7, 1, 6, 2, 3, 8, 9, 10, 11, 12):
        loads[i].start()

    def x_copy(step, peer, slot):
        return pltpu.make_async_remote_copy(
            src_ref=send_f.at[step, peer],
            dst_ref=recv_f.at[step, slot],
            send_sem=x_send.at[step],
            recv_sem=x_recv.at[step],
            device_id=(peer, me_r),
            device_id_type=MESH,
        )

    def w_copy(step, peer, slot):
        return pltpu.make_async_remote_copy(
            src_ref=send_f.at[step, N + peer],
            dst_ref=recv_w.at[step, slot],
            send_sem=w_send.at[step],
            recv_sem=w_recv.at[step],
            device_id=(me_f, peer),
            device_id_type=MESH,
        )

    def v_copy(step, peer, slot):
        return pltpu.make_async_remote_copy(
            src_ref=send_r.at[step, peer],
            dst_ref=recv_f.at[step, N + slot],
            send_sem=v_send.at[step],
            recv_sem=v_recv.at[step],
            device_id=(me_f, peer),
            device_id_type=MESH,
        )

    def each_peer(me, act):
        for k in FAR_FIRST:
            act(lax.rem(me + k, N))

    before_f = lax.rem(me_f + N - 1, N)
    after_f = lax.rem(me_f + 1, N)
    before_r = lax.rem(me_r + N - 1, N)
    after_r = lax.rem(me_r + 1, N)
    sides = (
        ((me_f, after_r), 0),
        ((me_f, before_r), 1),
        ((after_f, me_r), 2),
        ((before_f, me_r), 3),
    )

    def diff_copies():
        return [
            pltpu.make_async_remote_copy(
                src_ref=diff_v,
                dst_ref=dh.at[side],
                send_sem=d_send,
                recv_sem=d_recv,
                device_id=device,
                device_id_type=MESH,
            )
            for device, side in sides
        ]

    def halo_copies(step):
        out = []
        for device, side in sides:
            part = (step, side % 2, pl.ds(0, TY) if side < 2 else pl.ds(TY, TX))
            out.append(
                pltpu.make_async_remote_copy(
                    src_ref=edge_out.at[part],
                    dst_ref=edge_in.at[part],
                    send_sem=h_send.at[step],
                    recv_sem=h_recv.at[step],
                    device_id=device,
                    device_id_type=MESH,
                )
            )
        return out

    def drain(ref, sem):
        pltpu.make_async_copy(ref, ref, sem).wait()

    def peers_of(ref, step):
        return ref.at[step, pl.ds(0, N - 1)]

    table[...] = jnp.zeros_like(table)
    loads[4].wait()
    loads[5].wait()
    table[0:N, 0:CAP] = inter_v[...].astype(F32)
    table[N : 2 * N, 0:CAP] = wall_v[...].astype(F32)

    def spread_slots(first, last):
        turned = jnp.transpose(table[...])
        for k in range(first, last):
            idxb[k * CAP : (k + 1) * CAP, :] = jnp.broadcast_to(
                turned[0:CAP, k : k + 1], (CAP, C)
            ).astype(jnp.int32)

    spread_slots(0, 2 * N)

    lane = lax.broadcasted_iota(jnp.int32, (128, 128), 1)
    sub = lax.broadcasted_iota(jnp.int32, (128, 128), 0)

    def build_gather(op, first, count):
        def turn(b, carry):
            node = decode(idxb[rows(b + first, 128), :])
            for h in range(NODES // 128):
                op[rows(b, 128), h * 128 : (h + 1) * 128] = one_hot(node == lane + h * 128)
            return carry

        lax.fori_loop(0, count, turn, 0)

    def build_scatter(op, first, count):
        def turn(b, carry):
            for j in range(count):
                node = jnp.broadcast_to(
                    rowb[(first + j) * 8 : (first + j) * 8 + 1, :], (128, 128)
                )
                op[rows(b, 128), j * 128 : (j + 1) * 128] = one_hot(node == sub + b * 128)
            return carry

        lax.fori_loop(0, NODES // 128, turn, 0)

    build_gather(g_op, 0, 8)

    loads[0].wait()
    loads[13].wait()
    for a in range(2):
        lens[a : a + 1, :] = jnp.full((1, C), len_s[a], jnp.int32)

    def mask_turn(b, carry):
        node = lax.broadcasted_iota(jnp.int32, (BLK, C), 0) + b * BLK
        for a in range(2):
            value = conc_in[a, rows(b, BLK), :].astype(F32)
            conc2[rows(b, BLK), a * C : (a + 1) * C] = jnp.where(
                node < len_s[a], value, 0.0
            ).astype(BF16)
        return carry

    lax.fori_loop(0, NODES // BLK, mask_turn, 0)

    def gather(op, source, first, dest, step, part):
        for begin in range(part * N * CAP, (part + 1) * N * CAP, BLK):
            found = jnp.dot(op[begin : begin + BLK, :], source[...], preferred_element_type=F32)
            high = idxb[first + begin : first + begin + BLK, :] >= NODES
            own = jnp.where(high, found[:, C:], found[:, :C]).astype(BF16)
            dest[step, begin // CAP : (begin + BLK) // CAP] = own.reshape(BLK // CAP, CAP, C)

    def send_crossing(step):
        each_peer(me_f, lambda peer: x_copy(step, peer, me_f).start())
        recv_f[step, me_f] = send_f[step, me_f]

    def send_walls(step):
        each_peer(me_r, lambda peer: w_copy(step, peer, me_r).start())
        recv_w[step, me_r] = send_f[step, N + me_r]

    def send_rock(step):
        each_peer(me_r, lambda peer: v_copy(step, peer, me_r).start())
        recv_f[step, N + me_r] = send_r[step, me_r]

    gather(g_op, conc2, 0, send_f, 0, 0)
    gather(g_op, conc2, 0, send_f, 0, 1)
    loads[7].wait()

    s_here = jnp.sqrt(diff_v[...])
    table[0:TX, :] = s_here
    turned = jnp.transpose(table[...])
    for x in range(TX):
        s_bc[x] = jnp.broadcast_to(turned[:, x : x + 1], (TY, C))

    def put_state(step, x, state):
        scaled = s_bc[x] * state
        r_ref[x] = state
        w_ref[step, x + 1, 8 : 8 + TY, :] = scaled
        ye[0, pl.ds(x, 1), :] = scaled[TY - 1 :, :]
        ye[1, pl.ds(x, 1), :] = scaled[:1, :]
        half, low = divmod(x, 8)
        rock2[low * TY : (low + 1) * TY, half * C : (half + 1) * C] = state.astype(BF16)

    def edges(step):
        edge_out[step, :, TY:, :] = ye[...].astype(BF16)
        edge_out[step, 0, :TY, :] = w_ref[step, TX, 8 : 8 + TY, :].astype(BF16)
        edge_out[step, 1, :TY, :] = w_ref[step, 1, 8 : 8 + TY, :].astype(BF16)

    loads[1].wait()
    for x in range(TX):
        put_state(0, x, jnp.transpose(rock_in[:, x, :]))
    edges(0)

    pl.semaphore_wait(barrier, 2 * (N - 1))
    for copy in diff_copies() + halo_copies(0):
        copy.start()
    send_crossing(0)
    send_walls(0)
    loads[6].wait()
    table[2 * N : 3 * N, 0:CAP] = cells_v[...].astype(F32)
    spread_slots(2 * N, 3 * N)
    build_gather(r_op, 8, 4)

    for j in range(12):
        row = jnp.zeros((8, 128), F32)
        kind, first = divmod(4 * j, N)
        source = (inter_v, wall_v, cells_v)[kind]
        pieces = [source[first + i : first + i + 1, :] for i in range(4)]
        rowb[j * 8 : j * 8 + 1, :] = decode(jnp.concatenate(pieces, axis=1))
    build_scatter(rt_op, 8, 4)
    build_scatter(gt_op, 0, 8)

    def product():
        for a in range(2):
            conc = conc2[:, a * C : (a + 1) * C]
            for first in range(0, NODES, BLK):
                part = slice(first, first + BLK)
                acc[a, part, :] = conc[part, :].astype(F32) + jnp.dot(
                    flux_v[a, part, :], conc, preferred_element_type=F32
                )

    loads[2].wait()
    product()
    gather(r_op, rock2, 2 * N * CAP, send_r, 0, 0)
    send_rock(0)

    drain(dh, d_recv)
    xrow = lax.broadcasted_iota(jnp.int32, (TX, TY), 0)
    ycol = lax.broadcasted_iota(jnp.int32, (TX, TY), 1)
    side_s = jnp.sqrt(dh[...])
    first_r, last_r = me_r == 0, me_r == N - 1
    first_f, last_f = me_f == 0, me_f == N - 1
    down_x = jnp.where(first_r, 0.0, side_s[0, TX - 1 :, :])
    up_x = jnp.where(last_r, 0.0, side_s[1, :1, :])
    down_y = jnp.where(first_f, 0.0, pltpu.roll(side_s[2], 1, 1))
    up_y = jnp.where(last_f, 0.0, pltpu.roll(side_s[3], TY - 1, 1))
    total = jnp.where(xrow == 0, down_x, pltpu.roll(s_here, 1, 0))
    total = total + jnp.where(xrow == TX - 1, up_x, pltpu.roll(s_here, TX - 1, 0))
    total = total + jnp.where(ycol == 0, down_y, pltpu.roll(s_here, 1, 1))
    total = total + jnp.where(ycol == TY - 1, up_y, pltpu.roll(s_here, TY - 1, 1))
    table[0:TX, :] = s_here * total
    turned = jnp.transpose(table[...])
    for x in range(TX):
        t_bc[x] = jnp.broadcast_to(turned[:, x : x + 1], (TY, C))

    for i in (8, 9, 10, 11, 12):
        loads[i].wait()
    cross_rate = cross_v[...]
    wall_rate = wrate_v[...]

    def flux_of(rate, recv, send, dest, step, first, begin):
        def turn(p, carry):
            value = rate * (recv[step, p].astype(F32) - send[step, p].astype(F32))
            high = idxb[rows(first + p, CAP), :] >= NODES
            dest[rows(p, CAP), :C] = jnp.where(high, 0.0, value).astype(BF16)
            dest[rows(p, CAP), C:] = jnp.where(high, value, 0.0).astype(BF16)
            return carry

        lax.fori_loop(begin, begin + N, turn, 0)

    def inflow(begin, last):
        for first in range(0, NODES, BLK):
            part = slice(first, first + BLK)
            slots = slice(begin * CAP, (begin + N) * CAP)
            came = jnp.dot(gt_op[part, slots], f2[slots, :], preferred_element_type=F32)
            for a in range(2):
                total = acc[a, part, :] + came[:, a * C : (a + 1) * C]
                if last:
                    mixed2[part, a * C : (a + 1) * C] = total.astype(BF16)
                else:
                    acc[a, part, :] = total

    def solve_walls(step, last):
        drain(peers_of(recv_f, step), v_recv.at[step])
        flux_of(wall_rate, recv_f, send_f, f2, step, 0, N)
        inflow(N, last)

    def solve_crossing(step, last):
        drain(peers_of(recv_f, step), x_recv.at[step])
        flux_of(cross_rate, recv_f, send_f, f2, step, 0, 0)
        inflow(0, last)

    def advance():
        loads[3].wait()
        for a in range(2):
            for first in range(0, NODES, BLK):
                conc2[first : first + BLK, a * C : (a + 1) * C] = solved_rows(
                    inv_v, mixed2, lens, a, first, BLK
                )

    comp_rate = comp_v[...]
    cap = cap_v[...]
    aff = aff_v[...]

    def stencil(step):
        drain(edge_in.at[step], h_recv.at[step])
        w_ref[step, 0, 8 : 8 + TY, :] = jnp.where(first_r, 0.0, edge_in[step, 0, :TY, :].astype(F32))
        w_ref[step, TX + 1, 8 : 8 + TY, :] = jnp.where(last_r, 0.0, edge_in[step, 1, :TY, :].astype(F32))
        yh[0] = jnp.where(first_f, 0.0, edge_in[step, 0, TY:, :].astype(F32))
        yh[1] = jnp.where(last_f, 0.0, edge_in[step, 1, TY:, :].astype(F32))
        for x in range(TX):
            w_ref[step, x + 1, 7:8, :] = yh[0, x : x + 1, :]
            w_ref[step, x + 1, 8 + TY : 9 + TY, :] = yh[1, x : x + 1, :]
        for x in range(TX):
            old = r_ref[x]
            around = (w_ref[step, x, 8 : 8 + TY, :] + w_ref[step, x + 2, 8 : 8 + TY, :]) + (
                w_ref[step, x + 1, 7 : 7 + TY, :] + w_ref[step, x + 1, 9 : 9 + TY, :]
            )
            diffusion = comp_rate * (s_bc[x] * around - t_bc[x] * old)
            root = 1.0 + aff * jnp.abs(old)
            square = root * root
            share = square / (square + cap)
            r_ref[x] = old + diffusion * share
            fac[x] = share

    def absorb(step):
        drain(peers_of(recv_w, step), w_recv.at[step])
        flux_of(wall_rate, recv_w, send_r, fr2, step, 2 * N, 0)
        if step < STEPS - 1:
            for low in range(0, 8, 2):
                for x, new in absorbed(rt_op, fr2, r_ref, fac, low):
                    put_state(step + 1, x, new)

    stencil(0)
    absorb(0)
    edges(1)
    for copy in halo_copies(1):
        copy.start()
    gather(r_op, rock2, 2 * N * CAP, send_r, 1, 0)
    send_rock(1)
    solve_crossing(0, False)
    solve_walls(0, True)
    advance()
    gather(g_op, conc2, 0, send_f, 1, 0)
    send_crossing(1)
    gather(g_op, conc2, 0, send_f, 1, 1)
    send_walls(1)
    product()
    stencil(1)
    solve_walls(1, False)
    absorb(1)
    solve_crossing(1, True)

    drain(dh, d_send)
    for step in range(STEPS):
        drain(peers_of(send_f, step), x_send.at[step])
        drain(peers_of(send_f, step), w_send.at[step])
        drain(peers_of(send_r, step), v_send.at[step])
        drain(edge_out.at[step], h_send.at[step])


def finish(
    inv_v, mixed2, lens, r_ref, fac, fr2, rt_op, conc_h, rock_h, conc_v, rock_v, sem
):
    def solve_part(a, first):
        conc_v[a, first : first + BLK, :] = solved_rows(inv_v, mixed2, lens, a, first, BLK)

    for low in range(0, 8, 2):
        for x, new in absorbed(rt_op, fr2, r_ref, fac, low):
            rock_v[:, x, :] = jnp.transpose(new)
        solve_part(0, low // 2 * BLK)
    copies = [
        pltpu.make_async_copy(rock_v, rock_h, sem.at[0]),
        pltpu.make_async_copy(conc_v.at[0], conc_h.at[0], sem.at[1]),
    ]
    copies[0].start()
    copies[1].start()
    for first in range(0, NODES, BLK):
        solve_part(1, first)
        part = (1, pl.ds(first, BLK))
        copies.append(
            pltpu.make_async_copy(conc_v.at[part], conc_h.at[part], sem.at[len(copies)])
        )
        copies[-1].start()
    for copy in copies:
        copy.wait()


def local(
    frac_conc,
    frac_len,
    frac_flux,
    frac_inverse,
    inter_rows,
    wall_rows,
    wall_cells,
    rock_conc,
    rock_diff,
    comp_rate,
    cross_rate,
    wall_rate,
    sorb_cap,
    sorb_aff,
):
    any_spec = pl.BlockSpec(memory_space=pl.ANY)
    vmem = pl.BlockSpec(memory_space=pltpu.VMEM)
    dma = pltpu.SemaphoreType.DMA
    V = pltpu.VMEM
    def stay(x):
        return pltpu.with_memory_space_constraint(x, pltpu.HBM)

    passed = pl.pallas_call(
        kernel,
        out_shape=(
            V(frac_inverse.shape, BF16),
            V((NODES, 2 * C), BF16),
            V((8, C), jnp.int32),
            V((TX, TY, C), F32),
            V((TX, TY, C), F32),
            V((N * CAP, 2 * C), BF16),
            V((NODES, N * CAP), BF16),
        ),
        in_specs=[any_spec] * 14,
        out_specs=(vmem,) * 7,
        scratch_shapes=[
            pltpu.SMEM((2,), jnp.int32),
            V((N, CAP), jnp.int32),
            V((N, CAP), jnp.int32),
            V((N, CAP), jnp.int32),
            V((TX, TY), F32),
            V((1, C), F32),
            V((1, C), F32),
            V((1, C), F32),
            V((1, C), F32),
            V((1, C), F32),
            V((2, NODES, C), BF16),
            V((2, NODES, NODES), BF16),
            V((C, TX, TY), F32),
            V((NODES, 2 * C), BF16),
            V((2, NODES, C), F32),
            V((128, 128), F32),
            V((3 * N * CAP, C), jnp.int32),
            V((12 * 8, 128), jnp.int32),
            V((2 * N * CAP, NODES), BF16),
            V((NODES, 2 * N * CAP), BF16),
            V((N * CAP, NODES), BF16),
            V((2 * N * CAP, 2 * C), BF16),
            V((STEPS, 2 * N, CAP, C), BF16),
            V((STEPS, 2 * N, CAP, C), BF16),
            V((STEPS, N, CAP, C), BF16),
            V((STEPS, N, CAP, C), BF16),
            V((NODES, 2 * C), BF16),
            V((TX, TY, C), F32),
            V((TX, TY, C), F32),
            V((STEPS, TX + 2, TY + 16, C), F32),
            V((4, TX, TY), F32),
            V((2, TX, C), F32),
            V((2, TX, C), F32),
            V((STEPS, 2, TY + TX, C), BF16),
            V((STEPS, 2, TY + TX, C), BF16),
            dma((14,)),
            dma((STEPS,)),
            dma((STEPS,)),
            dma((STEPS,)),
            dma((STEPS,)),
            dma((STEPS,)),
            dma((STEPS,)),
            dma((STEPS,)),
            dma((STEPS,)),
            dma(()),
            dma(()),
        ],
        compiler_params=pltpu.CompilerParams(
            collective_id=0, has_side_effects=True, vmem_limit_bytes=36 << 20
        ),
        name="tracer_steps",
    )(
        stay(frac_conc),
        stay(frac_len),
        stay(frac_flux),
        stay(frac_inverse),
        stay(inter_rows[0, 0]),
        stay(wall_rows[0, 0]),
        stay(wall_cells[0, 0]),
        stay(rock_conc),
        stay(rock_diff),
        stay(comp_rate.reshape(1, C)),
        stay(cross_rate.reshape(1, C)),
        stay(wall_rate.reshape(1, C)),
        stay(sorb_cap.reshape(1, C)),
        stay(sorb_aff.reshape(1, C)),
    )
    return pl.pallas_call(
        finish,
        out_shape=(
            jax.ShapeDtypeStruct(frac_conc.shape, BF16),
            jax.ShapeDtypeStruct(rock_conc.shape, F32),
        ),
        in_specs=[vmem] * 7,
        out_specs=(any_spec, any_spec),
        scratch_shapes=[V(frac_conc.shape, BF16), V(rock_conc.shape, F32), dma((2 + NODES // BLK,))],
        compiler_params=pltpu.CompilerParams(vmem_limit_bytes=8 << 20),
        name="finish",
    )(*passed)


def solution(mesh):
    return jax.shard_map(
        local,
        mesh=mesh,
        in_specs=(
            P(("frac", "rock"), None, None),
            P(("frac", "rock")),
            P(("frac", "rock"), None, None),
            P(("frac", "rock"), None, None),
            P("frac", "rock", None, None),
            P("frac", "rock", None, None),
            P("frac", "rock", None, None),
            P(None, "rock", "frac"),
            P("rock", "frac"),
            P(),
            P(),
            P(),
            P(),
            P(),
        ),
        out_specs=(P(("frac", "rock"), None, None), P(None, "rock", "frac")),
        check_vma=False,
    )
```

```python
import functools

import jax
import jax.numpy as jnp
from jax import lax
from jax.experimental import pallas as pl
from jax.experimental.pallas import tpu as pltpu
from jax.sharding import PartitionSpec as P

STEPS = 2
N = 16
CAP = 32
C = 128
NODES = 1024
TX = 16
TY = 128
F32 = jnp.float32
BF16 = jnp.bfloat16
MESH = pl.DeviceIdType.MESH
BLK = 256


def rows(b, size):
    return pl.ds(pl.multiple_of(b * size, size), size)


def one_hot(hit):
    return jnp.where(hit, 1.0, 0.0).astype(BF16)


def decode(v):
    return jnp.where(v < 0, -1, v & (NODES - 1))


FAR_FIRST = sorted(range(1, N), key=lambda k: abs(k - N // 2))


def solved_rows(inv_v, mixed2, lens, a, first, count):
    solved = jnp.dot(
        inv_v[a, first : first + count, :],
        mixed2[:, a * C : (a + 1) * C],
        preferred_element_type=F32,
    )
    node = lax.broadcasted_iota(jnp.int32, (count, C), 0) + first
    return jnp.where(node < lens[a : a + 1, :], solved, 0.0).astype(BF16)


def absorbed(rt_op, fr2, r_ref, fac, low):
    gain = jnp.dot(rt_op[low * TY : (low + 2) * TY, :], fr2[...], preferred_element_type=F32)
    for half in range(2):
        for i in range(2):
            x = half * 8 + low + i
            brought = gain[i * TY : (i + 1) * TY, half * C : (half + 1) * C]
            yield x, r_ref[x] + fac[x] * brought


def kernel(
    conc_h,
    len_h,
    flux_h,
    inv_h,
    inter_h,
    wall_h,
    cells_h,
    rock_h,
    diff_h,
    comp_h,
    cross_h,
    wrate_h,
    cap_h,
    aff_h,
    inv_v,
    mixed2,
    lens,
    r_ref,
    fac,
    fr2,
    rt_op,
    len_s,
    inter_v,
    wall_v,
    cells_v,
    diff_v,
    comp_v,
    cross_v,
    wrate_v,
    cap_v,
    aff_v,
    conc_in,
    flux_v,
    rock_in,
    conc2,
    acc,
    table,
    idxb,
    rowb,
    g_op,
    gt_op,
    r_op,
    f2,
    send_f,
    recv_f,
    send_r,
    recv_w,
    rock2,
    s_bc,
    t_bc,
    w_ref,
    dh,
    ye,
    yh,
    edge_out,
    edge_in,
    load_sem,
    x_send,
    x_recv,
    w_send,
    w_recv,
    v_send,
    v_recv,
    h_send,
    h_recv,
    d_send,
    d_recv,
):
    me_f = lax.axis_index("frac")
    me_r = lax.axis_index("rock")

    loads = [
        pltpu.make_async_copy(src, dst, load_sem.at[i])
        for i, (src, dst) in enumerate(
            (
                (conc_h, conc_in),
                (rock_h, rock_in),
                (flux_h, flux_v),
                (inv_h, inv_v),
                (inter_h, inter_v),
                (wall_h, wall_v),
                (cells_h, cells_v),
                (diff_h, diff_v),
                (comp_h, comp_v),
                (cross_h, cross_v),
                (wrate_h, wrate_v),
                (cap_h, cap_v),
                (aff_h, aff_v),
                (len_h, len_s),
            )
        )
    ]
    barrier = pltpu.get_barrier_semaphore()

    loads[4].start()
    loads[5].start()
    for k in FAR_FIRST:
        pl.semaphore_signal(
            barrier, inc=1, device_id=(lax.rem(me_f + k, N), me_r), device_id_type=MESH
        )
    for k in FAR_FIRST:
        pl.semaphore_signal(
            barrier, inc=1, device_id=(me_f, lax.rem(me_r + k, N)), device_id_type=MESH
        )
    for i in (0, 13, 7, 1, 6, 2, 3, 8, 9, 10, 11, 12):
        loads[i].start()

    def x_copy(step, peer, slot):
        return pltpu.make_async_remote_copy(
            src_ref=send_f.at[step, peer],
            dst_ref=recv_f.at[step, slot],
            send_sem=x_send.at[step],
            recv_sem=x_recv.at[step],
            device_id=(peer, me_r),
            device_id_type=MESH,
        )

    def w_copy(step, peer, slot):
        return pltpu.make_async_remote_copy(
            src_ref=send_f.at[step, N + peer],
            dst_ref=recv_w.at[step, slot],
            send_sem=w_send.at[step],
            recv_sem=w_recv.at[step],
            device_id=(me_f, peer),
            device_id_type=MESH,
        )

    def v_copy(step, peer, slot):
        return pltpu.make_async_remote_copy(
            src_ref=send_r.at[step, peer],
            dst_ref=recv_f.at[step, N + slot],
            send_sem=v_send.at[step],
            recv_sem=v_recv.at[step],
            device_id=(me_f, peer),
            device_id_type=MESH,
        )

    def each_peer(me, act):
        for k in FAR_FIRST:
            act(lax.rem(me + k, N))

    before_f = lax.rem(me_f + N - 1, N)
    after_f = lax.rem(me_f + 1, N)
    before_r = lax.rem(me_r + N - 1, N)
    after_r = lax.rem(me_r + 1, N)
    sides = (
        ((me_f, after_r), 0),
        ((me_f, before_r), 1),
        ((after_f, me_r), 2),
        ((before_f, me_r), 3),
    )

    def diff_copies():
        out = []
        for device, side in sides:
            part = (pl.ds(TX - 8, 8), pl.ds(0, 8), pl.ds(0, TX), pl.ds(0, TX))[side]
            out.append(
                pltpu.make_async_remote_copy(
                    src_ref=diff_v.at[part],
                    dst_ref=dh.at[side, part],
                    send_sem=d_send,
                    recv_sem=d_recv,
                    device_id=device,
                    device_id_type=MESH,
                )
            )
        return out

    def halo_copies(step):
        out = []
        for device, side in sides:
            part = (step, side % 2, pl.ds(0, TY) if side < 2 else pl.ds(TY, TX))
            out.append(
                pltpu.make_async_remote_copy(
                    src_ref=edge_out.at[part],
                    dst_ref=edge_in.at[part],
                    send_sem=h_send.at[step],
                    recv_sem=h_recv.at[step],
                    device_id=device,
                    device_id_type=MESH,
                )
            )
        return out

    def drain(ref, sem):
        pltpu.make_async_copy(ref, ref, sem).wait()

    def peers_of(ref, step):
        return ref.at[step, pl.ds(0, N - 1)]

    table[...] = jnp.zeros_like(table)
    loads[4].wait()
    loads[5].wait()
    table[0:N, 0:CAP] = inter_v[...].astype(F32)
    table[N : 2 * N, 0:CAP] = wall_v[...].astype(F32)

    def spread_slots(first, last):
        turned = jnp.transpose(table[...])
        for k in range(first, last):
            idxb[k * CAP : (k + 1) * CAP, :] = jnp.broadcast_to(
                turned[0:CAP, k : k + 1], (CAP, C)
            ).astype(jnp.int32)

    spread_slots(0, 2 * N)

    lane = lax.broadcasted_iota(jnp.int32, (128, 128), 1)
    sub = lax.broadcasted_iota(jnp.int32, (128, 128), 0)

    def build_gather(op, first, count):
        def turn(b, carry):
            node = decode(idxb[rows(b + first, 128), :])
            for h in range(NODES // 128):
                op[rows(b, 128), h * 128 : (h + 1) * 128] = one_hot(node == lane + h * 128)
            return carry

        lax.fori_loop(0, count, turn, 0)

    def build_scatter(op, first, count):
        def turn(b, carry):
            for j in range(count):
                node = jnp.broadcast_to(
                    rowb[(first + j) * 8 : (first + j) * 8 + 1, :], (128, 128)
                )
                op[rows(b, 128), j * 128 : (j + 1) * 128] = one_hot(node == sub + b * 128)
            return carry

        lax.fori_loop(0, NODES // 128, turn, 0)

    build_gather(g_op, 0, 8)

    loads[0].wait()
    loads[13].wait()
    for a in range(2):
        lens[a : a + 1, :] = jnp.full((1, C), len_s[a], jnp.int32)

    def mask_turn(b, carry):
        node = lax.broadcasted_iota(jnp.int32, (BLK, C), 0) + b * BLK
        for a in range(2):
            value = conc_in[a, rows(b, BLK), :].astype(F32)
            conc2[rows(b, BLK), a * C : (a + 1) * C] = jnp.where(
                node < len_s[a], value, 0.0
            ).astype(BF16)
        return carry

    lax.fori_loop(0, NODES // BLK, mask_turn, 0)

    def gather(op, source, first, dest, step, part):
        for begin in range(part * N * CAP, (part + 1) * N * CAP, BLK):
            found = jnp.dot(op[begin : begin + BLK, :], source[...], preferred_element_type=F32)
            high = idxb[first + begin : first + begin + BLK, :] >= NODES
            own = jnp.where(high, found[:, C:], found[:, :C]).astype(BF16)
            dest[step, begin // CAP : (begin + BLK) // CAP] = own.reshape(BLK // CAP, CAP, C)

    def send_crossing(step):
        each_peer(me_f, lambda peer: x_copy(step, peer, me_f).start())
        recv_f[step, me_f] = send_f[step, me_f]

    def send_walls(step):
        each_peer(me_r, lambda peer: w_copy(step, peer, me_r).start())
        recv_w[step, me_r] = send_f[step, N + me_r]

    def send_rock(step):
        each_peer(me_r, lambda peer: v_copy(step, peer, me_r).start())
        recv_f[step, N + me_r] = send_r[step, me_r]

    gather(g_op, conc2, 0, send_f, 0, 0)
    gather(g_op, conc2, 0, send_f, 0, 1)
    loads[7].wait()

    s_here = jnp.sqrt(diff_v[...])
    table[0:TX, :] = s_here
    turned = jnp.transpose(table[...])
    for x in range(TX):
        s_bc[x] = jnp.broadcast_to(turned[:, x : x + 1], (TY, C))

    def put_state(step, x, state):
        scaled = s_bc[x] * state
        r_ref[x] = state
        w_ref[step, x + 1, 8 : 8 + TY, :] = scaled
        ye[0, pl.ds(x, 1), :] = scaled[TY - 1 :, :]
        ye[1, pl.ds(x, 1), :] = scaled[:1, :]
        half, low = divmod(x, 8)
        rock2[low * TY : (low + 1) * TY, half * C : (half + 1) * C] = state.astype(BF16)

    def edges(step):
        edge_out[step, :, TY:, :] = ye[...].astype(BF16)
        edge_out[step, 0, :TY, :] = w_ref[step, TX, 8 : 8 + TY, :].astype(BF16)
        edge_out[step, 1, :TY, :] = w_ref[step, 1, 8 : 8 + TY, :].astype(BF16)

    loads[1].wait()
    for x in range(TX):
        put_state(0, x, jnp.transpose(rock_in[:, x, :]))
    edges(0)

    pl.semaphore_wait(barrier, 2 * (N - 1))
    for copy in diff_copies() + halo_copies(0):
        copy.start()
    send_crossing(0)
    send_walls(0)
    loads[6].wait()
    table[2 * N : 3 * N, 0:CAP] = cells_v[...].astype(F32)
    spread_slots(2 * N, 3 * N)
    build_gather(r_op, 8, 4)

    for j in range(12):
        row = jnp.zeros((8, 128), F32)
        kind, first = divmod(4 * j, N)
        source = (inter_v, wall_v, cells_v)[kind]
        pieces = [source[first + i : first + i + 1, :] for i in range(4)]
        rowb[j * 8 : j * 8 + 1, :] = decode(jnp.concatenate(pieces, axis=1))
    build_scatter(rt_op, 8, 4)
    build_scatter(gt_op, 0, 8)

    def product():
        for a in range(2):
            conc = conc2[:, a * C : (a + 1) * C]
            for first in range(0, NODES, BLK):
                part = slice(first, first + BLK)
                acc[a, part, :] = conc[part, :].astype(F32) + jnp.dot(
                    flux_v[a, part, :], conc, preferred_element_type=F32
                )

    loads[2].wait()
    product()
    gather(r_op, rock2, 2 * N * CAP, send_r, 0, 0)
    send_rock(0)

    drain(dh.at[pl.ds(0, 3)], d_recv)
    xrow = lax.broadcasted_iota(jnp.int32, (TX, TY), 0)
    ycol = lax.broadcasted_iota(jnp.int32, (TX, TY), 1)
    first_r, last_r = me_r == 0, me_r == N - 1
    first_f, last_f = me_f == 0, me_f == N - 1
    down_x = jnp.where(first_r, 0.0, jnp.sqrt(dh[0, TX - 1 :, :]))
    up_x = jnp.where(last_r, 0.0, jnp.sqrt(dh[1, :1, :]))
    down_y = jnp.where(first_f, 0.0, pltpu.roll(jnp.sqrt(dh[2]), 1, 1))
    up_y = jnp.where(last_f, 0.0, pltpu.roll(jnp.sqrt(dh[3]), TY - 1, 1))
    total = jnp.where(xrow == 0, down_x, pltpu.roll(s_here, 1, 0))
    total = total + jnp.where(xrow == TX - 1, up_x, pltpu.roll(s_here, TX - 1, 0))
    total = total + jnp.where(ycol == 0, down_y, pltpu.roll(s_here, 1, 1))
    total = total + jnp.where(ycol == TY - 1, up_y, pltpu.roll(s_here, TY - 1, 1))
    table[0:TX, :] = s_here * total
    turned = jnp.transpose(table[...])
    for x in range(TX):
        t_bc[x] = jnp.broadcast_to(turned[:, x : x + 1], (TY, C))

    for i in (8, 9, 10, 11, 12):
        loads[i].wait()
    cross_rate = cross_v[...]
    wall_rate = wrate_v[...]

    def flux_of(rate, recv, send, dest, step, first, begin):
        for p in range(begin, begin + N, 4):
            part = slice(p * CAP, (p + 4) * CAP)
            here = slice((first + p) * CAP, (first + p + 4) * CAP)
            value = rate * (
                recv[step, p : p + 4].reshape(4 * CAP, C).astype(F32)
                - send[step, p : p + 4].reshape(4 * CAP, C).astype(F32)
            )
            high = idxb[here, :] >= NODES
            dest[part, :C] = jnp.where(high, 0.0, value).astype(BF16)
            dest[part, C:] = jnp.where(high, value, 0.0).astype(BF16)

    def inflow(begin, last):
        for first in range(0, NODES, BLK):
            part = slice(first, first + BLK)
            slots = slice(begin * CAP, (begin + N) * CAP)
            came = jnp.dot(gt_op[part, slots], f2[slots, :], preferred_element_type=F32)
            for a in range(2):
                total = acc[a, part, :] + came[:, a * C : (a + 1) * C]
                if last:
                    mixed2[part, a * C : (a + 1) * C] = total.astype(BF16)
                else:
                    acc[a, part, :] = total

    def solve_walls(step, last):
        drain(peers_of(recv_f, step), v_recv.at[step])
        flux_of(wall_rate, recv_f, send_f, f2, step, 0, N)
        inflow(N, last)

    def solve_crossing(step, last):
        drain(peers_of(recv_f, step), x_recv.at[step])
        flux_of(cross_rate, recv_f, send_f, f2, step, 0, 0)
        inflow(0, last)

    def advance():
        loads[3].wait()
        for a in range(2):
            for first in range(0, NODES, BLK):
                conc2[first : first + BLK, a * C : (a + 1) * C] = solved_rows(
                    inv_v, mixed2, lens, a, first, BLK
                )

    comp_rate = comp_v[...]
    cap = cap_v[...]
    aff = aff_v[...]

    def stencil(step):
        drain(edge_in.at[step], h_recv.at[step])
        w_ref[step, 0, 8 : 8 + TY, :] = jnp.where(first_r, 0.0, edge_in[step, 0, :TY, :].astype(F32))
        w_ref[step, TX + 1, 8 : 8 + TY, :] = jnp.where(last_r, 0.0, edge_in[step, 1, :TY, :].astype(F32))
        yh[0] = jnp.where(first_f, 0.0, edge_in[step, 0, TY:, :].astype(F32))
        yh[1] = jnp.where(last_f, 0.0, edge_in[step, 1, TY:, :].astype(F32))
        for x in range(TX):
            w_ref[step, x + 1, 7:8, :] = yh[0, x : x + 1, :]
            w_ref[step, x + 1, 8 + TY : 9 + TY, :] = yh[1, x : x + 1, :]
        for x in range(TX):
            old = r_ref[x]
            around = (w_ref[step, x, 8 : 8 + TY, :] + w_ref[step, x + 2, 8 : 8 + TY, :]) + (
                w_ref[step, x + 1, 7 : 7 + TY, :] + w_ref[step, x + 1, 9 : 9 + TY, :]
            )
            diffusion = comp_rate * (s_bc[x] * around - t_bc[x] * old)
            root = 1.0 + aff * jnp.abs(old)
            square = root * root
            share = square / (square + cap)
            r_ref[x] = old + diffusion * share
            fac[x] = share

    def absorb(step):
        drain(peers_of(recv_w, step), w_recv.at[step])
        flux_of(wall_rate, recv_w, send_r, fr2, step, 2 * N, 0)
        if step < STEPS - 1:
            for low in range(0, 8, 2):
                for x, new in absorbed(rt_op, fr2, r_ref, fac, low):
                    put_state(step + 1, x, new)

    stencil(0)
    absorb(0)
    edges(1)
    for copy in halo_copies(1):
        copy.start()
    gather(r_op, rock2, 2 * N * CAP, send_r, 1, 0)
    send_rock(1)
    solve_crossing(0, False)
    solve_walls(0, True)
    advance()
    gather(g_op, conc2, 0, send_f, 1, 0)
    send_crossing(1)
    gather(g_op, conc2, 0, send_f, 1, 1)
    send_walls(1)
    product()
    stencil(1)
    solve_walls(1, False)
    absorb(1)
    solve_crossing(1, True)

    drain(dh.at[pl.ds(0, 3)], d_send)
    for step in range(STEPS):
        drain(peers_of(send_f, step), x_send.at[step])
        drain(peers_of(send_f, step), w_send.at[step])
        drain(peers_of(send_r, step), v_send.at[step])
        drain(edge_out.at[step], h_send.at[step])


def finish(
    inv_v, mixed2, lens, r_ref, fac, fr2, rt_op, conc_h, rock_h, conc_v, rock_v, sem
):
    def solve_part(a, first):
        conc_v[a, first : first + BLK, :] = solved_rows(inv_v, mixed2, lens, a, first, BLK)

    for low in range(0, 8, 2):
        for x, new in absorbed(rt_op, fr2, r_ref, fac, low):
            rock_v[:, x, :] = jnp.transpose(new)
        solve_part(0, low // 2 * BLK)
    copies = [
        pltpu.make_async_copy(rock_v, rock_h, sem.at[0]),
        pltpu.make_async_copy(conc_v.at[0], conc_h.at[0], sem.at[1]),
    ]
    copies[0].start()
    copies[1].start()
    for first in range(0, NODES, BLK):
        solve_part(1, first)
        part = (1, pl.ds(first, BLK))
        copies.append(
            pltpu.make_async_copy(conc_v.at[part], conc_h.at[part], sem.at[len(copies)])
        )
        copies[-1].start()
    for copy in copies:
        copy.wait()


def local(
    frac_conc,
    frac_len,
    frac_flux,
    frac_inverse,
    inter_rows,
    wall_rows,
    wall_cells,
    rock_conc,
    rock_diff,
    comp_rate,
    cross_rate,
    wall_rate,
    sorb_cap,
    sorb_aff,
):
    any_spec = pl.BlockSpec(memory_space=pl.ANY)
    vmem = pl.BlockSpec(memory_space=pltpu.VMEM)
    dma = pltpu.SemaphoreType.DMA
    V = pltpu.VMEM
    def stay(x):
        return pltpu.with_memory_space_constraint(x, pltpu.HBM)

    passed = pl.pallas_call(
        kernel,
        out_shape=(
            V(frac_inverse.shape, BF16),
            V((NODES, 2 * C), BF16),
            V((8, C), jnp.int32),
            V((TX, TY, C), F32),
            V((TX, TY, C), F32),
            V((N * CAP, 2 * C), BF16),
            V((NODES, N * CAP), BF16),
        ),
        in_specs=[any_spec] * 14,
        out_specs=(vmem,) * 7,
        scratch_shapes=[
            pltpu.SMEM((2,), jnp.int32),
            V((N, CAP), jnp.int32),
            V((N, CAP), jnp.int32),
            V((N, CAP), jnp.int32),
            V((TX, TY), F32),
            V((1, C), F32),
            V((1, C), F32),
            V((1, C), F32),
            V((1, C), F32),
            V((1, C), F32),
            V((2, NODES, C), BF16),
            V((2, NODES, NODES), BF16),
            V((C, TX, TY), F32),
            V((NODES, 2 * C), BF16),
            V((2, NODES, C), F32),
            V((128, 128), F32),
            V((3 * N * CAP, C), jnp.int32),
            V((12 * 8, 128), jnp.int32),
            V((2 * N * CAP, NODES), BF16),
            V((NODES, 2 * N * CAP), BF16),
            V((N * CAP, NODES), BF16),
            V((2 * N * CAP, 2 * C), BF16),
            V((STEPS, 2 * N, CAP, C), BF16),
            V((STEPS, 2 * N, CAP, C), BF16),
            V((STEPS, N, CAP, C), BF16),
            V((STEPS, N, CAP, C), BF16),
            V((NODES, 2 * C), BF16),
            V((TX, TY, C), F32),
            V((TX, TY, C), F32),
            V((STEPS, TX + 2, TY + 16, C), F32),
            V((4, TX, TY), F32),
            V((2, TX, C), F32),
            V((2, TX, C), F32),
            V((STEPS, 2, TY + TX, C), BF16),
            V((STEPS, 2, TY + TX, C), BF16),
            dma((14,)),
            dma((STEPS,)),
            dma((STEPS,)),
            dma((STEPS,)),
            dma((STEPS,)),
            dma((STEPS,)),
            dma((STEPS,)),
            dma((STEPS,)),
            dma((STEPS,)),
            dma(()),
            dma(()),
        ],
        compiler_params=pltpu.CompilerParams(
            collective_id=0, has_side_effects=True, vmem_limit_bytes=36 << 20
        ),
        name="tracer_steps",
    )(
        stay(frac_conc),
        stay(frac_len),
        stay(frac_flux),
        stay(frac_inverse),
        stay(inter_rows[0, 0]),
        stay(wall_rows[0, 0]),
        stay(wall_cells[0, 0]),
        stay(rock_conc),
        stay(rock_diff),
        stay(comp_rate.reshape(1, C)),
        stay(cross_rate.reshape(1, C)),
        stay(wall_rate.reshape(1, C)),
        stay(sorb_cap.reshape(1, C)),
        stay(sorb_aff.reshape(1, C)),
    )
    return pl.pallas_call(
        finish,
        out_shape=(
            jax.ShapeDtypeStruct(frac_conc.shape, BF16),
            jax.ShapeDtypeStruct(rock_conc.shape, F32),
        ),
        in_specs=[vmem] * 7,
        out_specs=(any_spec, any_spec),
        scratch_shapes=[V(frac_conc.shape, BF16), V(rock_conc.shape, F32), dma((2 + NODES // BLK,))],
        compiler_params=pltpu.CompilerParams(vmem_limit_bytes=8 << 20),
        name="finish",
    )(*passed)


def solution(mesh):
    return jax.shard_map(
        local,
        mesh=mesh,
        in_specs=(
            P(("frac", "rock"), None, None),
            P(("frac", "rock")),
            P(("frac", "rock"), None, None),
            P(("frac", "rock"), None, None),
            P("frac", "rock", None, None),
            P("frac", "rock", None, None),
            P("frac", "rock", None, None),
            P(None, "rock", "frac"),
            P("rock", "frac"),
            P(),
            P(),
            P(),
            P(),
            P(),
        ),
        out_specs=(P(("frac", "rock"), None, None), P(None, "rock", "frac")),
        check_vma=False,
    )
```
